32 devices in a mesh: ty: 8 (over z, x), tx: 4 (over y, core).
Axes of the slice: x: 2, y: 2, z: 4, core: 2. Of those that a mesh axis runs over, the one named last changes fastest.
Arguments:
- specimen: float32 [2, 2048, 4096], P(None, 'ty', 'tx'), may hold values from -5 to 5
- probe_modes: float32 [4, 2, 128, 128], replicated, may hold values from -0.75 to 0.75
- patterns: float32 [256, 128, 128], P(('ty', 'tx')), may hold values from 0.25 to 2.5
- tile_row: int32 [256], P(('ty', 'tx')), may hold values from 0 to 7, as said below
- row_offset: int32 [256], P(('ty', 'tx')), may hold values from 0 to 128
- col_offset: int32 [256], P(('ty', 'tx')), may hold values from 0 to 896
Outputs:
- specimen_out: float32 [2, 2048, 4096], P(None, 'ty', 'tx')
- probe_out: float32 [4, 2, 128, 128], replicated
The draws below stay inside these ranges and needn't reach their ends.
Inputs may be any that keep to these rules, and one draw needn't show every extreme that they name: `tile_row`: each index of ty+tx holds 8 consecutive positions. At most 2 of one device's positions name the same tile row, and for every index of tx some tile row is named exactly 2 times by each device with that tx index.
All inputs are finite; a program needn't handle non-finite values.
Results may differ from the reference program's by a relative error of at most 0.0001.
Values sent between devices are 32-bit elements; how exact they have to be, the bound alone decides.
A program may use at most 192 MiB of HBM per device.

```python
import math
import jax
import jax.numpy as jnp
from jax import lax

PATCH = 128
MODES = 4
TR = 256
TC = 1024
P_DEV = 8
ITERS = 2
GRID_ROWS = 8
GRID_COLS = 4
CAP = 2
NPOS = 256
OBJ_R = 2048
OBJ_C = 4096


def draw_tile_row(key, part):
    devices_all = GRID_ROWS * GRID_COLS
    slot_total = GRID_ROWS * CAP
    key_hot = jax.random.fold_in(key, 11)
    key_pref = jax.random.fold_in(key, 23)
    key_jitter = jax.random.fold_in(key, 37)
    key_order = jax.random.fold_in(key, 41)
    hot_rows = jax.random.randint(key_hot, (GRID_COLS,), 0, GRID_ROWS)
    preferences = jax.random.randint(key_pref, (GRID_COLS, GRID_ROWS), 0, 4)
    jitter_values = jax.random.randint(key_jitter, (devices_all, slot_total), 0, 4096)
    device_ids = jnp.arange(devices_all, dtype=jnp.int32)
    column_ids = device_ids % GRID_COLS
    slot_ids = jnp.arange(slot_total, dtype=jnp.int32)
    slot_rows = slot_ids // CAP
    pref_table = preferences[column_ids][:, slot_rows]
    scores = (pref_table * 4096 + jitter_values) * 256 + slot_ids[None, :]
    is_hot = slot_rows[None, :] == hot_rows[column_ids][:, None]
    scores = jnp.where(is_hot, 16777216 + slot_ids[None, :], scores)
    chosen = lax.top_k(scores, P_DEV)[1]
    chosen_rows = (chosen // CAP).astype(jnp.int32)
    order_keys = jax.random.randint(key_order, (devices_all, P_DEV), 0, 4096) * 64 + jnp.arange(P_DEV, dtype=jnp.int32)[None, :]
    ordering = jnp.argsort(order_keys, axis=1)
    shuffled = jnp.take_along_axis(chosen_rows, ordering, axis=1)
    return shuffled.reshape(-1).astype(jnp.int32)


def draw_probe_modes(key, part):
    key_amp = jax.random.fold_in(key, 5)
    key_phase = jax.random.fold_in(key, 7)
    lower_end = 0.8
    radius_frac = 0.42
    floor_level = 0.25
    counter = jnp.arange(PATCH, dtype=jnp.float32) - (PATCH - 1) / 2.0
    rho_sq = (counter[:, None] ** 2 + counter[None, :] ** 2) / (radius_frac * PATCH) ** 2
    envelope = floor_level + (1.0 - floor_level) * jnp.exp(-rho_sq ** 4)
    mode_weight = 0.75 * 0.68 ** jnp.arange(MODES, dtype=jnp.float32)
    amplitude = jax.random.uniform(key_amp, (MODES, PATCH, PATCH), jnp.float32, lower_end, 1.0)
    phases = jax.random.uniform(key_phase, (MODES, PATCH, PATCH), jnp.float32, -math.pi, math.pi)
    magnitude = mode_weight[:, None, None] * amplitude * envelope[None]
    return jnp.stack([magnitude * jnp.cos(phases), magnitude * jnp.sin(phases)], axis=1).astype(jnp.float32)


def place_ends(result, key, low, top_value):
    longest = result.shape.index(max(result.shape))
    spots = []
    for shift in (0, 1):
        where = [jax.random.randint(jax.random.fold_in(key, axis), (), 0, length) for axis, length in enumerate(result.shape)]
        where[longest] = (where[longest] + shift) % result.shape[longest]
        spots.append(tuple(where))
    return result.at[spots[0]].set(low).at[spots[1]].set(top_value)


def shard_levels(stream_key, dims, cuts, smallest, top_value):
    gain, own = 1.0, jax.random.fold_in(stream_key, 6)
    for dim, shards_of in cuts:
        steps = jnp.exp(jax.random.uniform(jax.random.fold_in(own, dim), (shards_of,), jnp.float32, smallest / len(cuts), top_value / len(cuts)))
        gain = gain * jnp.repeat(steps, dims[dim] // shards_of).reshape([-1 if axis == dim else 1 for axis in range(len(dims))])
    return gain


def gaussian(key, shape, deviation, most, split=(), kind=jnp.bfloat16):
    factor_of = shard_levels(key, shape, split, -0.22, 0.18) if split else 1.0
    array = jax.random.normal(key, shape, jnp.float32) * deviation * factor_of
    return jnp.minimum(jnp.maximum(array, -most), most).astype(kind)


def setup_inputs(seed: int = 0) -> dict:
    arg_keys = jax.random.split(jax.random.key(seed), 7)
    return {
        "specimen": gaussian(arg_keys[0], (2, OBJ_R, OBJ_C), 0.7, 5.0, ((1, 8), (2, 4)), jnp.float32),
        "probe_modes": draw_probe_modes(jax.random.fold_in(arg_keys[6], 71), 0),
        "patterns": jnp.clip(0.25 + 2.25 * jax.random.uniform(arg_keys[2], (NPOS, PATCH, PATCH), jnp.float32) ** shard_levels(arg_keys[2], (NPOS, PATCH, PATCH), ((0, 32),), -0.2, 0.2), 0.25, 2.5),
        "tile_row": draw_tile_row(jax.random.fold_in(arg_keys[6], 71), 0),
        "row_offset": place_ends(jax.random.randint(arg_keys[4], (NPOS,), 0, TR - PATCH + 1), jax.random.fold_in(arg_keys[4], 1), 0, TR - PATCH).astype(jnp.int32),
        "col_offset": place_ends(jax.random.randint(arg_keys[5], (NPOS,), 0, TC - PATCH + 1), jax.random.fold_in(arg_keys[5], 1), 0, TC - PATCH).astype(jnp.int32),
    }


AMP_FLOOR = 0.3
OBJ_STEP = 1.0
SMALL_EPS = 1e-06

def position_terms(window_cut, probe_modes, intensity):
    window_c = window_cut[0] + 1j * window_cut[1]
    modes_c = probe_modes[:, 0] + 1j * probe_modes[:, 1]
    exit_wave = modes_c * window_c[None]
    far_field = jnp.fft.fft2(exit_wave, norm='ortho')
    model_power = lax.optimization_barrier(jnp.sum(jnp.real(far_field) ** 2 + jnp.imag(far_field) ** 2, axis=0))
    factor = jnp.sqrt(intensity) / jnp.maximum(jnp.sqrt(model_power), AMP_FLOOR) - 1.0
    change = jnp.fft.ifft2(far_field * factor[None], norm='ortho')
    grad_window = lax.optimization_barrier(jnp.sum(jnp.conj(modes_c) * change, axis=0))
    grad_modes = jnp.conj(window_c)[None] * change
    lighting = window_cut[0] ** 2 + window_cut[1] ** 2
    return (jnp.stack([jnp.real(grad_window), jnp.imag(grad_window)]), jnp.stack([jnp.real(grad_modes), jnp.imag(grad_modes)], axis=1), lighting)

def reference(specimen, probe_modes, patterns, tile_row, row_offset, col_offset):
    index_all = jnp.arange(NPOS, dtype=jnp.int32)
    band_index = index_all // P_DEV % GRID_COLS
    rows_at = (tile_row * TR + row_offset).astype(jnp.int32)
    cols_at = (band_index * TC + col_offset).astype(jnp.int32)
    anchor = jnp.int32(0)
    for sweep_index in range(ITERS):
        current = specimen

        def visit_one(running, inputs):
            grad_sum, light_sum = running
            row_at, col_at, intensity = inputs
            window_cut = lax.dynamic_slice(current, (anchor, row_at, col_at), (2, PATCH, PATCH))
            grad_window, grad_modes, lighting = position_terms(window_cut, probe_modes, intensity)
            return ((grad_sum + grad_modes, light_sum + lighting), grad_window)
        initial = (jnp.zeros((MODES, 2, PATCH, PATCH), jnp.float32), jnp.zeros((PATCH, PATCH), jnp.float32))
        (grad_sum, light_sum), grad_windows = lax.scan(visit_one, initial, (rows_at, cols_at, patterns))
        probe_power = lax.optimization_barrier(jnp.sum(probe_modes[:, 0] ** 2 + probe_modes[:, 1] ** 2, axis=0))
        obj_scale = OBJ_STEP / (jnp.max(probe_power) + SMALL_EPS)

        def deposit(position, running_field):
            row_at = rows_at[position]
            col_at = cols_at[position]
            region = lax.dynamic_slice(running_field, (anchor, row_at, col_at), (2, PATCH, PATCH))
            return lax.dynamic_update_slice(running_field, region + obj_scale * grad_windows[position], (anchor, row_at, col_at))
        specimen = lax.fori_loop(0, NPOS, deposit, current)
        probe_modes = probe_modes + grad_sum / (jnp.max(light_sum) + SMALL_EPS)
    return (specimen, probe_modes)
```

```python
import functools
import math

import jax
import jax.numpy as jnp
import ml_dtypes
import numpy as np
from jax import lax
from jax.experimental import pallas as pl
from jax.experimental.pallas import tpu as pltpu
from jax.sharding import PartitionSpec as P

ITERS = 2
AMP_FLOOR = 0.3
OBJ_STEP = 1.0
SMALL_EPS = 1e-06

VMEM = pltpu.VMEM
SMEM = pltpu.SMEM
LIMIT = 56 * 1024 * 1024
MESH = pl.DeviceIdType.MESH


def dft_tables(length):
    counter = np.arange(length, dtype=np.int64)
    angles = (counter[:, None] * counter[None, :] % length) * (2.0 * math.pi / length)
    cos = np.cos(angles) / math.sqrt(length)
    sin = np.sin(angles) / math.sqrt(length)
    one = np.block([[cos, sin], [-sin, cos]])

    def parts(table):
        high = table.astype(ml_dtypes.bfloat16)
        return high, (table - high.astype(np.float64)).astype(ml_dtypes.bfloat16)

    lefts, rights = [], []
    for table in (one, one.T):
        high, low = parts(table)
        lefts.append(np.concatenate([high, low, high], axis=1))
        high, low = parts(table.T)
        rights.append(np.concatenate([high, high, low], axis=0))
    return np.stack(lefts), np.stack(rights)


def split(values):
    high = values.astype(jnp.bfloat16)
    low = (values - high.astype(jnp.float32)).astype(jnp.bfloat16)
    return high, low


def dot(a, b):
    return jnp.dot(a, b, preferred_element_type=jnp.float32)


def left(table, values):
    high, low = split(values)
    return dot(table, jnp.concatenate([high, high, low], axis=0))


def right(values, table):
    high, low = split(values)
    return dot(jnp.concatenate([high, low, high], axis=1), table)


def blocks2(a, b, c, d):
    return jnp.concatenate(
        [jnp.concatenate([a, b], axis=1), jnp.concatenate([c, d], axis=1)], axis=0
    )


def flip(index, mask):
    out, bit = index, 1
    while bit <= mask:
        if mask & bit:
            out = out + bit * (1 - 2 * lax.rem(index // bit, 2))
        bit *= 2
    return out


class Plan:
    def __init__(self, nty, ntx, own, window, modes, rows, cols):
        self.nty, self.ntx, self.ny = nty, ntx, ntx // 2
        self.own, self.window, self.modes = own, window, modes
        self.cap = max(2, 2 * own // nty)
        self.slots = nty * self.cap
        self.tiles = window // 8
        self.row_blocks, self.col_blocks = rows // 8, cols // window
        self.count = 2 * modes * self.tiles
        self.half = self.count // 2
        self.quarter = self.half // self.ny
        self.chunk = self.quarter // nty
        self.light = self.tiles // nty


def program_kernel(
    plan,
    tile_ref, row_ref, col_ref, pat_any, spec_any, probe_any, left_any, right_any,
    spec_out, probe_out,
    pat, spec, next_spec, left_t, right_t, probe, grad, light, shifted,
    send_pat, got_pat, send_head, got_head, head, col_tab, wave_w, far, power_ref,
    half_in, part, y_in, piece, ty_in, lt_in, lx_in, lm_send, lm_in,
    load_sem, head_sem, out_sem,
    hs, hr, ps, pr, ls, lr, xs, xr, ms, mr, cs, cr, ys, yr, ts, tr, tgs, tgr, ygs, ygr, cgs, cgr,
):
    f32 = jnp.float32
    nty, ny, cap, window, modes = plan.nty, plan.ny, plan.cap, plan.window, plan.modes
    tiles, chunk, quarter, half_n = plan.tiles, plan.chunk, plan.quarter, plan.half
    ty, tx = lax.axis_index("ty"), lax.axis_index("tx")
    core, y = lax.rem(tx, 2), tx // 2
    ty_dev = {d: {"ty": flip(ty, d)} for d in range(1, nty)}
    tx_dev = {d: {"tx": flip(tx, d)} for d in range(1, plan.ntx)}
    mate = tx_dev[1]

    barrier = pltpu.get_barrier_semaphore()
    for device in list(ty_dev.values()) + list(tx_dev.values()):
        pl.semaphore_signal(barrier, inc=1, device_id=device, device_id_type=MESH)

    loads = [
        pltpu.make_async_copy(src, dst, load_sem.at[k])
        for k, (src, dst) in enumerate((
            (pat_any, pat), (probe_any, probe.at[0]), (left_any, left_t), (right_any, right_t),
        ))
    ] + [
        pltpu.make_async_copy(
            spec_any.at[:, :, :, pl.ds(j * window, window)], spec.at[:, :, j], load_sem.at[4 + j]
        )
        for j in range(plan.col_blocks)
    ]
    for copy in loads:
        copy.start()

    def send(src, dst, s, r, device):
        copy = pltpu.make_async_remote_copy(
            src_ref=src, dst_ref=dst, send_sem=s, recv_sem=r, device_id=device, device_id_type=MESH
        )
        copy.start()
        return copy

    lane = lax.broadcasted_iota(jnp.int32, (8, window), 1)
    picks = {}
    for d in range(nty):
        tile = flip(ty, d)
        seen = jnp.int32(0)
        place = [jnp.int32(0)] * cap
        valid = [jnp.int32(0)] * cap
        for p in range(plan.own):
            hit = (tile_ref[p] == tile).astype(jnp.int32)
            for r in range(cap):
                take = hit * (seen == r).astype(jnp.int32)
                place[r] = place[r] + take * p
                valid[r] = valid[r] + take
            seen = seen + hit
        vector = jnp.zeros((8, window), jnp.int32)
        for r in range(cap):
            for k, value in enumerate((row_ref[place[r]], col_ref[place[r]], valid[r])):
                vector = jnp.where(lane == 3 * r + k, value, vector)
        if d == 0:
            got_head[0] = vector
        else:
            send_head[d] = vector
        picks[d] = place

    shifted[...] = jnp.zeros_like(shifted)
    loads[0].wait()
    far_first = list(range(nty - 1, 0, -1))
    for d in [0] + far_first:
        for r in range(cap):
            root = jnp.sqrt(pat[picks[d][r]])
            if d == 0:
                got_pat[0, r] = root
            else:
                send_pat[d, r] = root

    pl.semaphore_wait(barrier, nty - 1 + plan.ntx - 1)
    heads = [
        send(send_head.at[d], got_head.at[d], hs.at[d], hr.at[d], ty_dev[d]) for d in far_first
    ]
    pats = [
        send(send_pat.at[d], got_pat.at[d], ps.at[d], pr.at[d], ty_dev[d]) for d in far_first
    ]
    for copy in loads[1:]:
        copy.wait()
    for copy in heads:
        copy.wait()
    to_scalar = pltpu.make_async_copy(got_head, head, head_sem.at[0])
    to_scalar.start()
    to_scalar.wait()

    def corner(s, k):
        return head[s // cap, 0, 3 * lax.rem(s, cap) + k]

    def cut_of(row, col):
        row0 = jnp.minimum(row // 8, plan.row_blocks - tiles - 1)
        col0 = jnp.minimum(col // window, plan.col_blocks - 2)
        return row0, col0, row - row0 * 8, col - col0 * window

    def tab(s, _):
        _, col0, _, _ = cut_of(corner(s, 0), corner(s, 1))
        for j in range(plan.col_blocks):
            col_tab[s * plan.col_blocks + j] = jnp.where((j >= col0) & (j <= col0 + 1), j - col0 + 1, 0)
        return 0

    lax.fori_loop(0, plan.slots, tab, 0)

    def sweep(it):
        now = spec if it == 0 else next_spec
        light[...] = jnp.zeros_like(light)
        grad[...] = jnp.zeros_like(grad)

        def plane(m, k):
            base = (2 * m + k) * tiles
            return probe[it, base:base + tiles].reshape(window, window)

        total_power = jnp.zeros((window, window), f32)
        for m in range(modes):
            total_power = total_power + (plane(m, 0) ** 2 + plane(m, 1) ** 2)
        scale = OBJ_STEP / (jnp.max(total_power, keepdims=True) + SMALL_EPS)

        def forward(d, _):
            bright = jnp.zeros((window, window), f32)
            for r in range(cap):
                s = d * cap + r
                row0, col0, row_s, col_s = cut_of(head[d, 0, 3 * r], head[d, 0, 3 * r + 1])
                valid = head[d, 0, 3 * r + 2].astype(f32)
                sub8 = lax.broadcasted_iota(jnp.int32, (tiles, 8, window), 1)
                lane17 = lax.broadcasted_iota(jnp.int32, (tiles + 1, 8, window), 2)
                cut = []
                for k in range(2):
                    first = jnp.stack([now[k, row0 + a, col0] for a in range(tiles + 1)])
                    second = jnp.stack([now[k, row0 + a, col0 + 1] for a in range(tiles + 1)])
                    joined = jnp.where(lane17 < col_s, second, first)
                    joined = pltpu.roll(joined, lax.rem(window - col_s, window), 2)
                    turned = pltpu.roll(joined, lax.rem(8 - row_s, 8), 1)
                    picked = jnp.where(sub8 < 8 - row_s, turned[:tiles], turned[1:])
                    cut.append(picked.reshape(window, window) * valid)
                w_re, w_im = cut
                wave_w[s, 0] = w_re
                wave_w[s, 1] = w_im
                bright = bright + (w_re * w_re + w_im * w_im)
                power = jnp.zeros((window, window), f32)
                for pair in range(0, modes, 2):
                    waves = []
                    for m in (pair, pair + 1):
                        p_re, p_im = plane(m, 0), plane(m, 1)
                        waves.append(jnp.concatenate(
                            [p_re * w_re - p_im * w_im, p_re * w_im + p_im * w_re], axis=1
                        ))
                    mid = right(jnp.concatenate(waves, axis=0), right_t[0])
                    mid = blocks2(
                        mid[:window, :window], mid[window:, :window],
                        mid[:window, window:], mid[window:, window:],
                    )
                    spread = left(left_t[0], mid)
                    far[s, pair // 2] = spread
                    square = spread[:window] ** 2 + spread[window:] ** 2
                    power = power + (square[:, :window] + square[:, window:])
                power_ref[s] = power
            light[...] += bright.reshape(tiles, 8, window)
            return 0

        lax.fori_loop(0, nty, forward, 0)

        def backward(d, _):
            if it == 0:
                @pl.when(d > 0)
                def _():
                    pltpu.make_async_remote_copy(
                        src_ref=send_pat.at[d], dst_ref=got_pat.at[d], send_sem=ps.at[d],
                        recv_sem=pr.at[d], device_id=ty_dev[1], device_id_type=MESH,
                    ).wait_recv()
            adds = [jnp.zeros((window, window), f32) for _ in range(2 * modes)]
            for r in range(cap):
                s = d * cap + r
                root = got_pat[d, r]
                factor = root / jnp.maximum(jnp.sqrt(power_ref[s]), AMP_FLOOR) - 1.0
                factor4 = blocks2(factor, factor, factor, factor)
                w_re, w_im = wave_w[s, 0], wave_w[s, 1]
                g_re = jnp.zeros((window, window), f32)
                g_im = jnp.zeros((window, window), f32)
                for pair in range(0, modes, 2):
                    mid = left(left_t[1], far[s, pair // 2] * factor4)
                    mid = blocks2(
                        mid[:window, :window], mid[window:, :window],
                        mid[:window, window:], mid[window:, window:],
                    )
                    back = right(mid, right_t[1])
                    for k, m in enumerate((pair, pair + 1)):
                        line = slice(k * window, (k + 1) * window)
                        b_re, b_im = back[line, :window], back[line, window:]
                        p_re, p_im = plane(m, 0), plane(m, 1)
                        g_re = g_re + (p_re * b_re + p_im * b_im)
                        g_im = g_im + (p_re * b_im - p_im * b_re)
                        adds[2 * m] = adds[2 * m] + (w_re * b_re + w_im * b_im)
                        adds[2 * m + 1] = adds[2 * m + 1] + (w_re * b_im - w_im * b_re)
                _, _, row_s, col_s = cut_of(head[d, 0, 3 * r], head[d, 0, 3 * r + 1])
                lane17 = lax.broadcasted_iota(jnp.int32, (tiles + 1, 8, window), 2)
                sub17 = lax.broadcasted_iota(jnp.int32, (tiles + 1, 8, window), 1)
                none = jnp.zeros((1, 8, window), f32)
                for k, g in enumerate((g_re, g_im)):
                    turned = pltpu.roll((g * scale).reshape(tiles, 8, window), lax.rem(row_s, 8), 1)
                    wide = jnp.where(
                        sub17 >= row_s,
                        jnp.concatenate([turned, none], axis=0),
                        jnp.concatenate([none, turned], axis=0),
                    )
                    wide = pltpu.roll(wide, lax.rem(col_s, window), 2)
                    shifted[s, k, 1:tiles + 2, 1] = jnp.where(lane17 >= col_s, wide, 0.0)
                    shifted[s, k, 1:tiles + 2, 2] = jnp.where(lane17 < col_s, wide, 0.0)
            for k in range(2 * modes):
                grad[k * tiles:(k + 1) * tiles] += adds[k].reshape(tiles, 8, window)
            return 0

        lax.fori_loop(0, nty, backward, 0)

        def deposit(low, high):
            target = next_spec

            def line(i, _):
                acc = [
                    [now[k, i, j] for j in range(plan.col_blocks)]
                    for k in range(2)
                ]
                for s in range(plan.slots):
                    row = head[s // cap, 0, 3 * (s % cap)]
                    row0 = jnp.minimum(row // 8, plan.row_blocks - tiles - 1)
                    at = jnp.where((i >= row0) & (i <= row0 + tiles), i - row0 + 1, 0)
                    for j in range(plan.col_blocks):
                        c = col_tab[s * plan.col_blocks + j]
                        for k in range(2):
                            acc[k][j] = acc[k][j] + shifted[s, k, at, c]
                for k in range(2):
                    for j in range(plan.col_blocks):
                        target[k, i, j] = acc[k][j]
                return 0

            lax.fori_loop(low, high, line, 0)

        copies = []

        def push(*args):
            copies.append(send(*args))
            return copies[-1]

        n = plan.light
        sent = [
            push(light.at[pl.ds(flip(ty, d) * n, n)], lt_in.at[it, d], ls.at[it, d], lr.at[it, d], ty_dev[d])
            for d in range(1, nty)
        ]
        for copy in sent:
            copy.wait()
        mine = light[pl.ds(ty * n, n)]
        for d in range(1, nty):
            mine = mine + lt_in[it, d]
        lx_in[it, 0] = mine
        sent = [
            push(lx_in.at[it, 0], lx_in.at[it, d], xs.at[it, d], xr.at[it, d], tx_dev[d])
            for d in range(1, plan.ntx)
        ]
        for copy in sent:
            copy.wait()
        for d in range(1, plan.ntx):
            mine = mine + lx_in[it, d]
        lm_in[it, 0] = jnp.max(mine, axis=0)
        sent = [
            push(lm_in.at[it, 0], lm_in.at[it, d], ms.at[it, d], mr.at[it, d], ty_dev[d])
            for d in range(1, nty)
        ]
        for copy in sent:
            copy.wait()
        bottom = jnp.max(jnp.max(lm_in[it], axis=0), keepdims=True) + SMALL_EPS

        order = list(range(1, ny)) + [0]
        halves = {}
        for e in order:
            k = flip(y, e)
            halves[e] = push(
                grad.at[pl.ds((1 - core) * half_n + k * quarter, quarter)],
                half_in.at[it, e], cs.at[it, e], cr.at[it, e], mate,
            )
        deposit(0, plan.row_blocks // 4)
        ysent = []
        for e in order:
            halves[e].wait()
            k = flip(y, e)
            part[it, e] = grad[pl.ds(core * half_n + k * quarter, quarter)] + half_in[it, e]
            if e:
                ysent.append(push(part.at[it, e], y_in.at[it, e], ys.at[it, e], yr.at[it, e], {"tx": k * 2 + core}))
        deposit(plan.row_blocks // 4, plan.row_blocks // 2)
        acc = part[it, 0]
        for e, copy in zip(order, ysent):
            copy.wait()
            acc = acc + y_in[it, e]
        piece[it] = acc
        sent = [
            push(piece.at[it, pl.ds(flip(ty, d) * chunk, chunk)], ty_in.at[it, d], ts.at[it, d], tr.at[it, d], ty_dev[d])
            for d in far_first
        ]
        deposit(plan.row_blocks // 2, plan.row_blocks * 3 // 4)
        for copy in sent:
            copy.wait()
        mine = piece[it, pl.ds(ty * chunk, chunk)]
        for d in range(1, nty):
            mine = mine + ty_in[it, d]
        at = core * half_n + y * quarter + ty * chunk
        probe[it + 1, pl.ds(at, chunk)] = probe[it, pl.ds(at, chunk)] + mine / bottom
        own = probe.at[it + 1, pl.ds(at, chunk)]
        sent = [push(own, own, tgs.at[it, d], tgr.at[it, d], ty_dev[d]) for d in far_first]
        deposit(plan.row_blocks * 3 // 4, plan.row_blocks)
        store = None
        if it == ITERS - 1:
            store = [
                pltpu.make_async_copy(
                    next_spec.at[:, :, j], spec_out.at[:, :, :, pl.ds(j * window, window)], out_sem.at[1 + j]
                )
                for j in range(plan.col_blocks)
            ]
            for copy in store:
                copy.start()
        for copy in sent:
            copy.wait()
        own = probe.at[it + 1, pl.ds(core * half_n + y * quarter, quarter)]
        gathered = [
            push(own, own, ygs.at[it, e], ygr.at[it, e], {"tx": flip(y, e) * 2 + core})
            for e in range(1, ny)
        ]
        last = [push(own, own, cgs.at[it, 0], cgr.at[it, 0], mate)]
        for e, copy in zip(range(1, ny), gathered):
            copy.wait()
            other = probe.at[it + 1, pl.ds(core * half_n + flip(y, e) * quarter, quarter)]
            last.append(push(other, other, cgs.at[it, e], cgr.at[it, e], mate))
        for copy in last:
            copy.wait()
        return store

    for it in range(ITERS):
        store = sweep(it)
    final = pltpu.make_async_copy(probe.at[ITERS], probe_out, out_sem.at[0])
    final.start()
    for copy in pats:
        copy.wait_send()
    for copy in store + [final]:
        copy.wait()


def shards(specimen, probe_modes, patterns, tile_row, row_offset, col_offset):
    own, window, _ = patterns.shape
    modes = probe_modes.shape[0]
    nty, ntx = lax.axis_size("ty"), lax.axis_size("tx")
    plan = Plan(nty, ntx, own, window, modes, specimen.shape[1], specimen.shape[2])
    lefts, rights = dft_tables(window)
    f32, dma = jnp.float32, pltpu.SemaphoreType.DMA
    shape = specimen.shape
    view = (2, plan.row_blocks, 8, shape[2])
    tiles, ny, cap = plan.tiles, plan.ny, plan.cap
    spec_view = (2, plan.row_blocks, plan.col_blocks, 8, window)
    probe_view = (plan.count, 8, window)
    pair = lambda n: dma((ITERS, n))
    scratch = [
        VMEM(patterns.shape, f32),
        VMEM(spec_view, f32),
        VMEM(spec_view, f32),
        VMEM(lefts.shape, jnp.bfloat16),
        VMEM(rights.shape, jnp.bfloat16),
        VMEM((ITERS + 1,) + probe_view, f32),
        VMEM(probe_view, f32),
        VMEM((tiles, 8, window), f32),
        VMEM((plan.slots, 2, tiles + 2, 3, 8, window), f32),
        VMEM((nty, cap, window, window), f32),
        VMEM((nty, cap, window, window), f32),
        VMEM((nty, 8, window), jnp.int32),
        VMEM((nty, 8, window), jnp.int32),
        SMEM((nty, 8, window), jnp.int32),
        SMEM((plan.slots * plan.col_blocks,), jnp.int32),
        VMEM((plan.slots, 2, window, window), f32),
        VMEM((plan.slots, modes // 2, 2 * window, 2 * window), f32),
        VMEM((plan.slots, window, window), f32),
        VMEM((ITERS, ny, plan.quarter, 8, window), f32),
        VMEM((ITERS, ny, plan.quarter, 8, window), f32),
        VMEM((ITERS, ny, plan.quarter, 8, window), f32),
        VMEM((ITERS, plan.quarter, 8, window), f32),
        VMEM((ITERS, nty, plan.chunk, 8, window), f32),
        VMEM((ITERS, nty, plan.light, 8, window), f32),
        VMEM((ITERS, ntx, plan.light, 8, window), f32),
        VMEM((8, window), f32),
        VMEM((ITERS, nty, 8, window), f32),
        dma((4 + plan.col_blocks,)), dma((1,)), dma((1 + plan.col_blocks,)),
        dma((nty,)), dma((nty,)), dma((nty,)), dma((nty,)),
        pair(nty), pair(nty), pair(ntx), pair(ntx), pair(nty), pair(nty),
        pair(ny), pair(ny), pair(ny), pair(ny), pair(nty), pair(nty),
        pair(nty), pair(nty), pair(ny), pair(ny), pair(ny), pair(ny),
    ]
    out, probe = pl.pallas_call(
        functools.partial(program_kernel, plan),
        out_shape=(jax.ShapeDtypeStruct(view, f32), jax.ShapeDtypeStruct(probe_view, f32)),
        in_specs=[pl.BlockSpec(memory_space=SMEM)] * 3 + [pl.BlockSpec(memory_space=pl.ANY)] * 5,
        out_specs=(pl.BlockSpec(memory_space=pl.ANY),) * 2,
        scratch_shapes=scratch,
        compiler_params=pltpu.CompilerParams(
            collective_id=0, has_side_effects=True, vmem_limit_bytes=LIMIT
        ),
        name="program",
    )(
        tile_row, row_offset, col_offset, patterns, specimen.reshape(view),
        probe_modes.reshape(probe_view), jnp.asarray(lefts), jnp.asarray(rights),
    )
    return out.reshape(shape), probe.reshape(probe_modes.shape)


def solution(mesh):
    placed = (
        P(None, "ty", "tx"),
        P(),
        P(("ty", "tx"), None, None),
        P(("ty", "tx")),
        P(("ty", "tx")),
        P(("ty", "tx")),
    )
    return jax.shard_map(
        shards, mesh=mesh, in_specs=placed, out_specs=(P(None, "ty", "tx"), P()), check_vma=False
    )
```

```python
import functools
import math

import jax
import jax.numpy as jnp
import ml_dtypes
import numpy as np
from jax import lax
from jax.experimental import pallas as pl
from jax.experimental.pallas import tpu as pltpu
from jax.sharding import PartitionSpec as P

ITERS = 2
AMP_FLOOR = 0.3
OBJ_STEP = 1.0
SMALL_EPS = 1e-06

VMEM = pltpu.VMEM
SMEM = pltpu.SMEM
LIMIT = 60 * 1024 * 1024
MESH = pl.DeviceIdType.MESH


def dft_tables(length):
    counter = np.arange(length, dtype=np.int64)
    angles = (counter[:, None] * counter[None, :] % length) * (2.0 * math.pi / length)
    cos = np.cos(angles) / math.sqrt(length)
    sin = np.sin(angles) / math.sqrt(length)
    one = np.block([[cos, sin], [-sin, cos]])

    def parts(table):
        high = table.astype(ml_dtypes.bfloat16)
        return high, (table - high.astype(np.float64)).astype(ml_dtypes.bfloat16)

    lefts, rights = [], []
    for table in (one, one.T):
        high, low = parts(table)
        lefts.append(np.concatenate([high, low, high], axis=1))
        high, low = parts(table.T)
        rights.append(np.concatenate([high, high, low], axis=0))
    return np.stack(lefts), np.stack(rights)


def split(values):
    high = values.astype(jnp.bfloat16)
    low = (values - high.astype(jnp.float32)).astype(jnp.bfloat16)
    return high, low


def dot(a, b):
    return jnp.dot(a, b, preferred_element_type=jnp.float32)


def left(table, values):
    high, low = split(values)
    return dot(table, jnp.concatenate([high, high, low], axis=0))


def right(values, table):
    high, low = split(values)
    return dot(jnp.concatenate([high, low, high], axis=1), table)


def blocks2(a, b, c, d):
    return jnp.concatenate(
        [jnp.concatenate([a, b], axis=1), jnp.concatenate([c, d], axis=1)], axis=0
    )


def flip(index, mask):
    out, bit = index, 1
    while bit <= mask:
        if mask & bit:
            out = out + bit * (1 - 2 * lax.rem(index // bit, 2))
        bit *= 2
    return out


class Plan:
    def __init__(self, nty, ntx, own, window, modes, rows, cols):
        self.nty, self.ntx, self.ny = nty, ntx, ntx // 2
        self.own, self.window, self.modes = own, window, modes
        self.cap = max(2, 2 * own // nty)
        self.slots = nty * self.cap
        self.units = self.slots // 2
        self.batch = self.units // 2
        while self.batch > 4:
            self.batch //= 2
        self.tiles = window // 8
        self.row_blocks, self.col_blocks = rows // 8, cols // window
        self.chips = nty * self.ny
        self.groups = max(1, min(modes, modes * self.tiles // self.chips))
        self.per = modes // self.groups
        self.chunk = self.per * self.tiles // self.chips
        self.light = self.tiles // nty


def program_kernel(
    plan,
    tile_ref, row_ref, col_ref, pat_any, spec_any, probe_any, left_any, right_any,
    spec_out, probe_out,
    pat, spec, next_spec, left_t, right_t, probe, grad, light, shifted,
    send_pat, got_pat, send_head, got_head, head, col_tab, wave_w, far, power_ref, gw,
    half_in, part, rs_in, lt_in, lx_in, lm_in,
    load_sem, head_sem, out_sem,
    hs, hr, ps, pr, ls, lr, xs, xr, ms, mr, cs, cr, rs, rr, gs, gr, bs, br,
):
    f32 = jnp.float32
    nty, ny, cap, window, modes = plan.nty, plan.ny, plan.cap, plan.window, plan.modes
    tiles, chunk, groups, per = plan.tiles, plan.chunk, plan.groups, plan.per
    ty, tx = lax.axis_index("ty"), lax.axis_index("tx")
    core, y = lax.rem(tx, 2), tx // 2
    ty_dev = {d: {"ty": flip(ty, d)} for d in range(1, nty)}
    tx_dev = {d: {"tx": flip(tx, d)} for d in range(1, plan.ntx)}
    mate = tx_dev[1]
    far_first = list(range(nty - 1, 0, -1))
    chips = [(a, e) for a in range(nty - 1, -1, -1) for e in range(ny - 1, -1, -1) if a or e]
    chip_dev = [{"ty": flip(ty, a), "tx": flip(tx, 2 * e)} for a, e in chips]
    chip_at = [flip(y, e) * nty + flip(ty, a) for a, e in chips]
    chip = y * nty + ty

    barrier = pltpu.get_barrier_semaphore()
    others = list(tx_dev.values()) + list(ty_dev.values())
    others += [dev for (a, e), dev in zip(chips, chip_dev) if a and e]
    for device in others:
        pl.semaphore_signal(barrier, inc=1, device_id=device, device_id_type=MESH)

    loads = [
        pltpu.make_async_copy(src, dst, load_sem.at[k])
        for k, (src, dst) in enumerate((
            (pat_any, pat), (probe_any.at[:, 0], probe.at[0, 0]), (probe_any.at[:, 1], probe.at[0, 1]),
            (left_any, left_t), (right_any, right_t),
        ))
    ] + [
        pltpu.make_async_copy(
            spec_any.at[:, :, :, pl.ds(j * window, window)], spec.at[:, :, j], load_sem.at[5 + j]
        )
        for j in range(plan.col_blocks)
    ]
    for copy in loads:
        copy.start()

    sent = []

    def remote(src, dst, s, r, device):
        return pltpu.make_async_remote_copy(
            src_ref=src, dst_ref=dst, send_sem=s, recv_sem=r, device_id=device, device_id_type=MESH
        )

    lane = lax.broadcasted_iota(jnp.int32, (8, window), 1)
    picks = {}
    for d in range(nty):
        tile = flip(ty, d)
        seen = jnp.int32(0)
        place = [jnp.int32(0)] * cap
        valid = [jnp.int32(0)] * cap
        for p in range(plan.own):
            hit = (tile_ref[p] == tile).astype(jnp.int32)
            for r in range(cap):
                take = hit * (seen == r).astype(jnp.int32)
                place[r] = place[r] + take * p
                valid[r] = valid[r] + take
            seen = seen + hit
        vector = jnp.zeros((8, window), jnp.int32)
        for r in range(cap):
            for k, value in enumerate((row_ref[place[r]], col_ref[place[r]], valid[r])):
                vector = jnp.where(lane == 3 * r + k, value, vector)
        if d == 0:
            got_head[0] = vector
        else:
            send_head[d] = vector
        picks[d] = place

    loads[0].wait()
    for d in [0] + far_first:
        for r in range(cap):
            root = jnp.sqrt(pat[picks[d][r]])
            if d == 0:
                got_pat[0, r] = root
            else:
                send_pat[d, r] = root

    pl.semaphore_wait(barrier, len(others))
    heads = [
        remote(send_head.at[d], got_head.at[d], hs.at[d], hr.at[d], ty_dev[d]) for d in far_first
    ]
    pats = [
        remote(send_pat.at[d], got_pat.at[d], ps.at[d], pr.at[d], ty_dev[d]) for d in far_first
    ]
    for copy in heads + pats:
        copy.start()
    shifted[...] = jnp.zeros_like(shifted)
    for copy in loads[1:]:
        copy.wait()
    for copy in heads:
        copy.wait()
    to_scalar = pltpu.make_async_copy(got_head, head, head_sem.at[0])
    to_scalar.start()
    to_scalar.wait()

    def cut_of(s, r):
        row, col = head[s // cap, 0, 3 * r], head[s // cap, 0, 3 * r + 1]
        row0 = jnp.minimum(row // 8, plan.row_blocks - tiles - 1)
        col0 = jnp.minimum(col // window, plan.col_blocks - 2)
        return row0, col0, row - row0 * 8, col - col0 * window

    def tab(s, _):
        _, col0, _, _ = cut_of(s, lax.rem(s, cap))
        for j in range(plan.col_blocks):
            col_tab[s * plan.col_blocks + j] = jnp.where((j >= col0) & (j <= col0 + 1), j - col0 + 1, 0)
        return 0

    lax.fori_loop(0, plan.slots, tab, 0)

    def windows(now):
        light[...] = jnp.zeros_like(light)

        def cut(s, _):
            r = lax.rem(s, cap)
            row0, col0, row_s, col_s = cut_of(s, r)
            valid = head[s // cap, 0, 3 * r + 2].astype(f32)
            sub8 = lax.broadcasted_iota(jnp.int32, (tiles, 8, window), 1)
            lane17 = lax.broadcasted_iota(jnp.int32, (tiles + 1, 8, window), 2)
            bright = jnp.zeros((tiles, 8, window), f32)
            for k in range(2):
                first = jnp.stack([now[k, row0 + a, col0] for a in range(tiles + 1)])
                second = jnp.stack([now[k, row0 + a, col0 + 1] for a in range(tiles + 1)])
                joined = jnp.where(lane17 < col_s, second, first)
                joined = pltpu.roll(joined, lax.rem(window - col_s, window), 2)
                turned = pltpu.roll(joined, lax.rem(8 - row_s, 8), 1)
                picked = jnp.where(sub8 < 8 - row_s, turned[:tiles], turned[1:]) * valid
                wave_w[s, k] = picked.reshape(window, window)
                bright = bright + picked * picked
            light[...] += bright
            return 0

        lax.fori_loop(0, plan.slots, cut, 0)

    def scale_of(it):
        total = jnp.zeros((tiles, 8, window), f32)
        for m in range(modes):
            total = total + (probe[it, 0, m] ** 2 + probe[it, 1, m] ** 2)
        return OBJ_STEP / (jnp.max(total.reshape(window, window), keepdims=True) + SMALL_EPS)

    def planes(it, m):
        return [probe[it, k, m].reshape(window, window) for k in range(2)]

    def turn(mids):
        rows = [
            jnp.concatenate([mid[half * window:(half + 1) * window, part * window:(part + 1) * window]
                             for half in range(2)], axis=1)
            for mid in mids for part in range(2)
        ]
        return rows

    def forward(it, m):
        p_re, p_im = planes(it, m)

        def some(b, _):
            for v in range(plan.batch):
                u = b * plan.batch + v
                waves = []
                for r in range(2):
                    w_re, w_im = wave_w[2 * u + r, 0], wave_w[2 * u + r, 1]
                    waves.append(jnp.concatenate(
                        [p_re * w_re - p_im * w_im, p_re * w_im + p_im * w_re], axis=1
                    ))
                mid = right(jnp.concatenate(waves, axis=0), right_t[0])
                spread = left(left_t[0], jnp.concatenate(turn([mid]), axis=0))
                far[m, u] = spread
                square = spread[:window] ** 2 + spread[window:] ** 2
                power_ref[u] = jnp.where(m == 0, square, power_ref[u] + square)
            return 0

        lax.fori_loop(0, plan.units // plan.batch, some, 0)

    def factors(it, low, high):
        def one(u, _):
            if it == 0:
                @pl.when(lax.rem(2 * u, cap) == 0)
                def _():
                    d = 2 * u // cap

                    @pl.when(d > 0)
                    def _():
                        remote(send_pat.at[d], got_pat.at[d], ps.at[d], pr.at[d], ty_dev[1]).wait_recv()
            d, r = 2 * u // cap, lax.rem(2 * u, cap)
            root = jnp.concatenate([got_pat[d, r], got_pat[d, r + 1]], axis=1)
            power_ref[u] = root / jnp.maximum(jnp.sqrt(power_ref[u]), AMP_FLOOR) - 1.0
            return 0

        lax.fori_loop(low, high, one, 0)

    def backward(it, m, low, high):
        p_re, p_im = planes(it, m)

        def some(b, _):
            add_re = jnp.zeros((window, window), f32)
            add_im = jnp.zeros((window, window), f32)
            for v in range(plan.batch):
                u = b * plan.batch + v
                factor = power_ref[u]
                mid = left(left_t[1], far[m, u] * jnp.concatenate([factor, factor], axis=0))
                back = right(jnp.concatenate(turn([mid]), axis=0), right_t[1])
                for r in range(2):
                    w_re, w_im = wave_w[2 * u + r, 0], wave_w[2 * u + r, 1]
                    line = slice(r * window, (r + 1) * window)
                    b_re, b_im = back[line, :window], back[line, window:]
                    add_re = add_re + (w_re * b_re + w_im * b_im)
                    add_im = add_im + (w_re * b_im - w_im * b_re)
                    g_re = p_re * b_re + p_im * b_im
                    g_im = p_re * b_im - p_im * b_re
                    gw[2 * u + r, 0] = jnp.where(m == 0, g_re, gw[2 * u + r, 0] + g_re)
                    gw[2 * u + r, 1] = jnp.where(m == 0, g_im, gw[2 * u + r, 1] + g_im)
            for k, add in enumerate((add_re, add_im)):
                add = add.reshape(tiles, 8, window)
                grad[k, m] = jnp.where(b == 0, add, grad[k, m] + add)
            return 0

        lax.fori_loop(low // plan.batch, high // plan.batch, some, 0)

    def shift(scale):
        def one(s, _):
            _, _, row_s, col_s = cut_of(s, lax.rem(s, cap))
            lane17 = lax.broadcasted_iota(jnp.int32, (tiles + 1, 8, window), 2)
            sub17 = lax.broadcasted_iota(jnp.int32, (tiles + 1, 8, window), 1)
            none = jnp.zeros((1, 8, window), f32)
            for k in range(2):
                turned = pltpu.roll((gw[s, k] * scale).reshape(tiles, 8, window), lax.rem(row_s, 8), 1)
                wide = jnp.where(
                    sub17 >= row_s,
                    jnp.concatenate([turned, none], axis=0),
                    jnp.concatenate([none, turned], axis=0),
                )
                wide = pltpu.roll(wide, lax.rem(col_s, window), 2)
                shifted[s, k, 1:tiles + 2, 1] = jnp.where(lane17 >= col_s, wide, 0.0)
                shifted[s, k, 1:tiles + 2, 2] = jnp.where(lane17 < col_s, wide, 0.0)
            return 0

        lax.fori_loop(0, plan.slots, one, 0)

    def deposit(now, low, high):
        def line(i, _):
            acc = [[now[k, i, j] for j in range(plan.col_blocks)] for k in range(2)]
            for s in range(plan.slots):
                row0, _, _, _ = cut_of(s, s % cap)
                at = jnp.where((i >= row0) & (i <= row0 + tiles), i - row0 + 1, 0)
                for j in range(plan.col_blocks):
                    c = col_tab[s * plan.col_blocks + j]
                    for k in range(2):
                        acc[k][j] = acc[k][j] + shifted[s, k, at, c]
            for k in range(2):
                for j in range(plan.col_blocks):
                    next_spec[k, i, j] = acc[k][j]
            return 0

        lax.fori_loop(low, high, line, 0)

    def light_one(it, d):
        n = plan.light
        return remote(
            light.at[pl.ds(flip(ty, d) * n, n)], lt_in.at[it, d], ls.at[it, d], lr.at[it, d], ty_dev[d]
        )

    def light_two(it, d):
        return remote(lx_in.at[it, 0], lx_in.at[it, d], xs.at[it, d], xr.at[it, d], tx_dev[d])

    def light_three(it, d):
        return remote(lm_in.at[it, 0], lm_in.at[it, d], ms.at[it, d], mr.at[it, d], ty_dev[d])

    def lighting(it, stage):
        if stage == 0:
            for d in range(1, nty):
                light_one(it, d).start()
        elif stage == 1:
            mine = light[pl.ds(ty * plan.light, plan.light)]
            for d in range(1, nty):
                light_one(it, d).wait()
                mine = mine + lt_in[it, d]
            lx_in[it, 0] = mine
            for d in range(1, plan.ntx):
                light_two(it, d).start()
        elif stage == 2:
            mine = lx_in[it, 0]
            for d in range(1, plan.ntx):
                light_two(it, d).wait()
                mine = mine + lx_in[it, d]
            lm_in[it, 0] = jnp.max(mine, axis=0)
            for d in range(1, nty):
                light_three(it, d).start()
        else:
            for d in range(1, nty):
                light_three(it, d).wait()

    def owned(at):
        return at * chunk // tiles, lax.rem(at * chunk, tiles)

    def step_a(it, g):
        return remote(
            grad.at[1 - core, pl.ds(g * per, per)], half_in.at[it, g], cs.at[it, g], cr.at[it, g], mate
        )

    def step_b(it, g, j):
        m, t = owned(chip_at[j])
        return remote(
            part.at[it, g, m, pl.ds(t, chunk)], rs_in.at[it, g, j], rs.at[it, g, j], rr.at[it, g, j], chip_dev[j]
        )

    def step_c(it, g, j):
        m, t = owned(chip)
        ref = probe.at[it + 1, core, g * per + m, pl.ds(t, chunk)]
        return remote(ref, ref, gs.at[it, g, j], gr.at[it, g, j], chip_dev[j])

    def step_d(it, g):
        ref = probe.at[it + 1, core, pl.ds(g * per, per)]
        return remote(ref, ref, bs.at[it, g], br.at[it, g], mate)

    def do_b(it, g):
        step_a(it, g).wait_recv()
        part[it, g] = grad[core, pl.ds(g * per, per)] + half_in[it, g]
        for j in range(len(chips)):
            step_b(it, g, j).start()

    def do_c(it, g, bottom):
        m, t = owned(chip)
        total = part[it, g, m, pl.ds(t, chunk)]
        for j in range(len(chips)):
            step_b(it, g, j).wait_recv()
            total = total + rs_in[it, g, j]
        at = g * per + m
        probe[it + 1, core, at, pl.ds(t, chunk)] = probe[it, core, at, pl.ds(t, chunk)] + total / bottom
        for j in range(len(chips)):
            step_c(it, g, j).start()

    def do_d(it, g):
        for j in range(len(chips)):
            step_c(it, g, j).wait_recv()
        step_d(it, g).start()

    def do_e(it, g):
        step_d(it, g).wait_recv()

    def close(it, g, _):
        step_a(it, g).wait_send()
        for j in range(len(chips)):
            step_b(it, g, j).wait_send()
            step_c(it, g, j).wait_send()
        step_d(it, g).wait_send()
        return 0

    windows(spec)
    lighting(0, 0)
    for it in range(ITERS):
        now = spec if it == 0 else next_spec

        def ahead(m, _):
            if it:
                g = m // per

                @pl.when(lax.rem(m, per) == 0)
                def _():
                    @pl.when(g + 1 < groups)
                    def _():
                        do_d(it - 1, g + 1)

                    do_e(it - 1, g)

            forward(it, m)
            return 0

        lax.fori_loop(0, modes // 2, ahead, 0)
        lighting(it, 1)
        lax.fori_loop(modes // 2, modes, ahead, 0)
        lighting(it, 2)
        if it:
            lax.fori_loop(0, groups, functools.partial(close, it - 1), 0)

        def back(low, high, m, _):
            backward(it, m, low, high)
            g = m // per

            @pl.when(lax.rem(m, per) == per - 1)
            def _():
                step_a(it, g).start()

                @pl.when(g > 0)
                def _():
                    do_b(it, g - 1)

            return 0

        if it == 0:
            half = plan.units // 2
            factors(it, 0, half)

            def early(m, _):
                backward(it, m, 0, half)
                return 0

            lax.fori_loop(0, modes, early, 0)
            lighting(it, 3)
            factors(it, half, plan.units)
            lax.fori_loop(0, modes, functools.partial(back, half, plan.units), 0)
        else:
            factors(it, 0, plan.units)
            lighting(it, 3)
            lax.fori_loop(0, modes, functools.partial(back, 0, plan.units), 0)
        bottom = jnp.max(jnp.max(lm_in[it], axis=0), keepdims=True) + SMALL_EPS
        shift(scale_of(it))
        do_b(it, groups - 1)
        for k in range(4):
            deposit(now, plan.row_blocks * k // 4, plan.row_blocks * (k + 1) // 4)
            if k < groups:
                do_c(it, k, bottom)
        for g in range(4, groups):
            do_c(it, g, bottom)
        if it + 1 < ITERS:
            windows(next_spec)
            lighting(it + 1, 0)
            do_d(it, 0)
    it = ITERS - 1
    store = [
        pltpu.make_async_copy(
            next_spec.at[:, :, j], spec_out.at[:, :, :, pl.ds(j * window, window)], out_sem.at[2 + j]
        )
        for j in range(plan.col_blocks)
    ]
    for copy in store:
        copy.start()
    for g in range(groups):
        do_d(it, g)
    for copy in pats:
        copy.wait_send()
    for g in range(groups):
        do_e(it, g)
    final = [
        pltpu.make_async_copy(probe.at[ITERS, k], probe_out.at[:, k], out_sem.at[k]) for k in range(2)
    ]
    for copy in final:
        copy.start()
    lax.fori_loop(0, groups, functools.partial(close, it), 0)
    for copy in store + final:
        copy.wait()


def shards(specimen, probe_modes, patterns, tile_row, row_offset, col_offset):
    own, window, _ = patterns.shape
    modes = probe_modes.shape[0]
    nty, ntx = lax.axis_size("ty"), lax.axis_size("tx")
    plan = Plan(nty, ntx, own, window, modes, specimen.shape[1], specimen.shape[2])
    lefts, rights = dft_tables(window)
    f32, dma = jnp.float32, pltpu.SemaphoreType.DMA
    shape = specimen.shape
    view = (2, plan.row_blocks, 8, shape[2])
    spec_view = (2, plan.row_blocks, plan.col_blocks, 8, window)
    tiles, cap, groups, others = plan.tiles, plan.cap, plan.groups, plan.chips - 1
    plane = (tiles, 8, window)
    probe_view = (modes, 2) + plane
    both = lambda *n: dma((ITERS,) + n)
    scratch = [
        VMEM(patterns.shape, f32),
        VMEM(spec_view, f32),
        VMEM(spec_view, f32),
        VMEM(lefts.shape, jnp.bfloat16),
        VMEM(rights.shape, jnp.bfloat16),
        VMEM((ITERS + 1, 2, modes) + plane, f32),
        VMEM((2, modes) + plane, f32),
        VMEM(plane, f32),
        VMEM((plan.slots, 2, tiles + 2, 3, 8, window), f32),
        VMEM((nty, cap, window, window), f32),
        VMEM((nty, cap, window, window), f32),
        VMEM((nty, 8, window), jnp.int32),
        VMEM((nty, 8, window), jnp.int32),
        SMEM((nty, 8, window), jnp.int32),
        SMEM((plan.slots * plan.col_blocks,), jnp.int32),
        VMEM((plan.slots, 2, window, window), f32),
        VMEM((modes, plan.units, 2 * window, 2 * window), f32),
        VMEM((plan.units, window, 2 * window), f32),
        VMEM((plan.slots, 2, window, window), f32),
        VMEM((ITERS, groups, plan.per) + plane, f32),
        VMEM((ITERS, groups, plan.per) + plane, f32),
        VMEM((ITERS, groups, others, plan.chunk, 8, window), f32),
        VMEM((ITERS, nty, plan.light, 8, window), f32),
        VMEM((ITERS, ntx, plan.light, 8, window), f32),
        VMEM((ITERS, nty, 8, window), f32),
        dma((5 + plan.col_blocks,)), dma((1,)), dma((2 + plan.col_blocks,)),
        dma((nty,)), dma((nty,)), dma((nty,)), dma((nty,)),
        both(nty), both(nty), both(ntx), both(ntx), both(nty), both(nty),
        both(groups), both(groups), both(groups, others), both(groups, others),
        both(groups, others), both(groups, others), both(groups), both(groups),
    ]
    out, probe = pl.pallas_call(
        functools.partial(program_kernel, plan),
        out_shape=(jax.ShapeDtypeStruct(view, f32), jax.ShapeDtypeStruct(probe_view, f32)),
        in_specs=[pl.BlockSpec(memory_space=SMEM)] * 3 + [pl.BlockSpec(memory_space=pl.ANY)] * 5,
        out_specs=(pl.BlockSpec(memory_space=pl.ANY),) * 2,
        scratch_shapes=scratch,
        compiler_params=pltpu.CompilerParams(
            collective_id=0, has_side_effects=True, vmem_limit_bytes=LIMIT
        ),
        name="program",
    )(
        tile_row, row_offset, col_offset, patterns, specimen.reshape(view),
        probe_modes.reshape(probe_view), jnp.asarray(lefts), jnp.asarray(rights),
    )
    return out.reshape(shape), probe.reshape(probe_modes.shape)


def solution(mesh):
    placed = (
        P(None, "ty", "tx"),
        P(),
        P(("ty", "tx"), None, None),
        P(("ty", "tx")),
        P(("ty", "tx")),
        P(("ty", "tx")),
    )
    return jax.shard_map(
        shards, mesh=mesh, in_specs=placed, out_specs=(P(None, "ty", "tx"), P()), check_vma=False
    )
```

```python
import functools
import math

import jax
import jax.numpy as jnp
import ml_dtypes
import numpy as np
from jax import lax
from jax.experimental import pallas as pl
from jax.experimental.pallas import tpu as pltpu
from jax.sharding import PartitionSpec as P

ITERS = 2
AMP_FLOOR = 0.3
OBJ_STEP = 1.0
SMALL_EPS = 1e-06
PARTS = 8

VMEM = pltpu.VMEM
SMEM = pltpu.SMEM
LIMIT = 60 * 1024 * 1024
MESH = pl.DeviceIdType.MESH


def dft_tables(length):
    counter = np.arange(length, dtype=np.int64)
    angles = (counter[:, None] * counter[None, :] % length) * (2.0 * math.pi / length)
    cos = np.cos(angles) / math.sqrt(length)
    sin = np.sin(angles) / math.sqrt(length)
    one = np.block([[cos, sin], [-sin, cos]])

    def parts(table):
        high = table.astype(ml_dtypes.bfloat16)
        return high, (table - high.astype(np.float64)).astype(ml_dtypes.bfloat16)

    lefts, rights = [], []
    for table in (one, one.T):
        high, low = parts(table)
        lefts.append(np.concatenate([high, low, high], axis=1))
        high, low = parts(table.T)
        rights.append(np.concatenate([high, high, low], axis=0))
    return np.stack(lefts), np.stack(rights)


def split(values):
    high = values.astype(jnp.bfloat16)
    low = (values - high.astype(jnp.float32)).astype(jnp.bfloat16)
    return high, low


def dot(a, b):
    return jnp.dot(a, b, preferred_element_type=jnp.float32)


def left(table, values):
    high, low = split(values)
    return dot(table, jnp.concatenate([high, high, low], axis=0))


def right(values, table):
    high, low = split(values)
    return dot(jnp.concatenate([high, low, high], axis=1), table)


def blocks2(a, b, c, d):
    return jnp.concatenate(
        [jnp.concatenate([a, b], axis=1), jnp.concatenate([c, d], axis=1)], axis=0
    )


def flip(index, mask):
    out, bit = index, 1
    while bit <= mask:
        if mask & bit:
            out = out + bit * (1 - 2 * lax.rem(index // bit, 2))
        bit *= 2
    return out


class Plan:
    def __init__(self, nty, ntx, own, window, modes, rows, cols):
        self.nty, self.ntx, self.ny = nty, ntx, ntx // 2
        self.own, self.window, self.modes = own, window, modes
        self.cap = max(2, 2 * own // nty)
        self.slots = nty * self.cap
        self.units = self.slots // 2
        self.batch = self.units // 2
        while self.batch > 4:
            self.batch //= 2
        self.wide = 2 * self.batch
        self.tiles = window // 8
        self.row_blocks, self.col_blocks = rows // 8, cols // window
        self.chips = nty * self.ny
        self.groups = max(1, min(modes, modes * self.tiles // self.chips))
        self.per = modes // self.groups
        self.chunk = self.per * self.tiles // self.chips
        self.light = self.tiles // nty


def program_kernel(
    plan,
    tile_ref, row_ref, col_ref, pat_any, spec_any, probe_any, left_any, right_any,
    spec_out, probe_out,
    pat, spec, next_spec, left_t, right_t, probe, grad, light, shifted,
    send_pat, got_pat, send_head, got_head, head, col_tab, wave_w, far, power_ref, gw,
    half_in, part, rs_in, lt_in, lx_in, lm_in,
    load_sem, head_sem, out_sem,
    hs, hr, ps, pr, ls, lr, xs, xr, ms, mr, cs, cr, rs, rr, gs, gr, bs, br,
):
    f32 = jnp.float32
    nty, ny, cap, window, modes = plan.nty, plan.ny, plan.cap, plan.window, plan.modes
    tiles, chunk, groups, per = plan.tiles, plan.chunk, plan.groups, plan.per
    ty, tx = lax.axis_index("ty"), lax.axis_index("tx")
    core, y = lax.rem(tx, 2), tx // 2
    ty_dev = {d: {"ty": flip(ty, d)} for d in range(1, nty)}
    tx_dev = {d: {"tx": flip(tx, d)} for d in range(1, plan.ntx)}
    mate = tx_dev[1]
    near_first = list(range(1, nty))
    chips = [(a, e) for a in range(nty - 1, -1, -1) for e in range(ny - 1, -1, -1) if a or e]
    chip_dev = [{"ty": flip(ty, a), "tx": flip(tx, 2 * e)} for a, e in chips]
    chip_at = [flip(y, e) * nty + flip(ty, a) for a, e in chips]
    chip = y * nty + ty

    barrier = pltpu.get_barrier_semaphore()
    others = list(tx_dev.values()) + list(ty_dev.values())
    others += [dev for (a, e), dev in zip(chips, chip_dev) if a and e]
    for device in others:
        pl.semaphore_signal(barrier, inc=1, device_id=device, device_id_type=MESH)

    loads = [
        pltpu.make_async_copy(src, dst, load_sem.at[k])
        for k, (src, dst) in enumerate((
            (pat_any, pat), (probe_any.at[:, 0], probe.at[0, 0]), (probe_any.at[:, 1], probe.at[0, 1]),
            (left_any, left_t), (right_any, right_t),
        ))
    ] + [
        pltpu.make_async_copy(
            spec_any.at[:, :, :, pl.ds(j * window, window)], spec.at[:, :, j], load_sem.at[5 + j]
        )
        for j in range(plan.col_blocks)
    ]
    for copy in loads:
        copy.start()

    sent = []

    def remote(src, dst, s, r, device):
        return pltpu.make_async_remote_copy(
            src_ref=src, dst_ref=dst, send_sem=s, recv_sem=r, device_id=device, device_id_type=MESH
        )

    lane = lax.broadcasted_iota(jnp.int32, (8, window), 1)
    picks = {}
    for d in range(nty):
        tile = flip(ty, d)
        seen = jnp.int32(0)
        place = [jnp.int32(0)] * cap
        valid = [jnp.int32(0)] * cap
        for p in range(plan.own):
            hit = (tile_ref[p] == tile).astype(jnp.int32)
            for r in range(cap):
                take = hit * (seen == r).astype(jnp.int32)
                place[r] = place[r] + take * p
                valid[r] = valid[r] + take
            seen = seen + hit
        vector = jnp.zeros((8, window), jnp.int32)
        for r in range(cap):
            for k, value in enumerate((row_ref[place[r]], col_ref[place[r]], valid[r])):
                vector = jnp.where(lane == 3 * r + k, value, vector)
        if d == 0:
            got_head[0] = vector
        else:
            send_head[d] = vector
        picks[d] = place

    loads[0].wait()
    for d in [0] + near_first:
        for r in range(cap):
            root = jnp.sqrt(pat[picks[d][r]])
            if d == 0:
                got_pat[0, r] = root
            else:
                send_pat[d, r] = root

    pl.semaphore_wait(barrier, len(others))
    heads = [
        remote(send_head.at[d], got_head.at[d], hs.at[d], hr.at[d], ty_dev[d]) for d in near_first
    ]
    pats = [
        remote(send_pat.at[d], got_pat.at[d], ps.at[d], pr.at[d], ty_dev[d]) for d in near_first
    ]
    for copy in heads + pats:
        copy.start()
    shifted[...] = jnp.zeros_like(shifted)
    for copy in loads[1:]:
        copy.wait()
    for copy in heads:
        copy.wait()
    to_scalar = pltpu.make_async_copy(got_head, head, head_sem.at[0])
    to_scalar.start()
    to_scalar.wait()

    def cut_of(s, r):
        row, col = head[s // cap, 0, 3 * r], head[s // cap, 0, 3 * r + 1]
        row0 = jnp.minimum(row // 8, plan.row_blocks - tiles - 1)
        col0 = jnp.minimum(col // window, plan.col_blocks - 2)
        return row0, col0, row - row0 * 8, col - col0 * window

    def tab(s, _):
        _, col0, _, _ = cut_of(s, lax.rem(s, cap))
        for j in range(plan.col_blocks):
            col_tab[s * plan.col_blocks + j] = jnp.where((j >= col0) & (j <= col0 + 1), j - col0 + 1, 0)
        return 0

    lax.fori_loop(0, plan.slots, tab, 0)

    def windows(now):
        light[...] = jnp.zeros_like(light)

        def cut(s, _):
            r = lax.rem(s, cap)
            row0, col0, row_s, col_s = cut_of(s, r)
            valid = head[s // cap, 0, 3 * r + 2].astype(f32)
            sub8 = lax.broadcasted_iota(jnp.int32, (tiles, 8, window), 1)
            lane17 = lax.broadcasted_iota(jnp.int32, (tiles + 1, 8, window), 2)
            bright = jnp.zeros((tiles, 8, window), f32)
            for k in range(2):
                first = jnp.stack([now[k, row0 + a, col0] for a in range(tiles + 1)])
                second = jnp.stack([now[k, row0 + a, col0 + 1] for a in range(tiles + 1)])
                joined = jnp.where(lane17 < col_s, second, first)
                joined = pltpu.roll(joined, lax.rem(window - col_s, window), 2)
                turned = pltpu.roll(joined, lax.rem(8 - row_s, 8), 1)
                picked = jnp.where(sub8 < 8 - row_s, turned[:tiles], turned[1:]) * valid
                wave_w[s, k] = picked.reshape(window, window)
                bright = bright + picked * picked
            light[...] += bright
            return 0

        lax.fori_loop(0, plan.slots, cut, 0)

    def scale_of(it):
        total = jnp.zeros((tiles, 8, window), f32)
        for m in range(modes):
            total = total + (probe[it, 0, m] ** 2 + probe[it, 1, m] ** 2)
        return OBJ_STEP / (jnp.max(total.reshape(window, window), keepdims=True) + SMALL_EPS)

    def planes(it, m):
        return [probe[it, k, m].reshape(window, window) for k in range(2)]

    def turn(mids):
        rows = [
            jnp.concatenate([mid[half * window:(half + 1) * window, part * window:(part + 1) * window]
                             for half in range(2)], axis=1)
            for mid in mids for part in range(2)
        ]
        return rows

    def forward(it, m):
        p_re, p_im = planes(it, m)

        def some(b, _):
            for v in range(plan.wide):
                u = b * plan.wide + v
                waves = []
                for r in range(2):
                    w_re, w_im = wave_w[2 * u + r, 0], wave_w[2 * u + r, 1]
                    waves.append(jnp.concatenate(
                        [p_re * w_re - p_im * w_im, p_re * w_im + p_im * w_re], axis=1
                    ))
                mid = right(jnp.concatenate(waves, axis=0), right_t[0])
                spread = left(left_t[0], jnp.concatenate(turn([mid]), axis=0))
                far[m, u] = spread
                square = spread[:window] ** 2 + spread[window:] ** 2
                power_ref[u] = jnp.where(m == 0, square, power_ref[u] + square)
            return 0

        lax.fori_loop(0, plan.units // plan.wide, some, 0)

    def factors(it, low, high):
        def one(u, _):
            if it == 0:
                @pl.when(lax.rem(2 * u, cap) == 0)
                def _():
                    d = 2 * u // cap

                    @pl.when(d > 0)
                    def _():
                        remote(send_pat.at[d], got_pat.at[d], ps.at[d], pr.at[d], ty_dev[1]).wait_recv()
            d, r = 2 * u // cap, lax.rem(2 * u, cap)
            root = jnp.concatenate([got_pat[d, r], got_pat[d, r + 1]], axis=1)
            power_ref[u] = root / jnp.maximum(jnp.sqrt(power_ref[u]), AMP_FLOOR) - 1.0
            return 0

        lax.fori_loop(low, high, one, 0)

    def backward(it, m, low, high):
        p_re, p_im = planes(it, m)
        batch = plan.batch if it == 0 else plan.wide

        def some(b, _):
            add_re = jnp.zeros((window, window), f32)
            add_im = jnp.zeros((window, window), f32)
            for v in range(batch):
                u = b * batch + v
                factor = power_ref[u]
                mid = left(left_t[1], far[m, u] * jnp.concatenate([factor, factor], axis=0))
                back = right(jnp.concatenate(turn([mid]), axis=0), right_t[1])
                for r in range(2):
                    w_re, w_im = wave_w[2 * u + r, 0], wave_w[2 * u + r, 1]
                    line = slice(r * window, (r + 1) * window)
                    b_re, b_im = back[line, :window], back[line, window:]
                    add_re = add_re + (w_re * b_re + w_im * b_im)
                    add_im = add_im + (w_re * b_im - w_im * b_re)
                    g_re = p_re * b_re + p_im * b_im
                    g_im = p_re * b_im - p_im * b_re
                    gw[2 * u + r, 0] = jnp.where(m == 0, g_re, gw[2 * u + r, 0] + g_re)
                    gw[2 * u + r, 1] = jnp.where(m == 0, g_im, gw[2 * u + r, 1] + g_im)
            for k, add in enumerate((add_re, add_im)):
                add = add.reshape(tiles, 8, window)
                grad[k, m] = jnp.where(b == 0, add, grad[k, m] + add)
            return 0

        lax.fori_loop(low // batch, high // batch, some, 0)

    def shift(scale):
        def one(s, _):
            _, _, row_s, col_s = cut_of(s, lax.rem(s, cap))
            lane17 = lax.broadcasted_iota(jnp.int32, (tiles + 1, 8, window), 2)
            sub17 = lax.broadcasted_iota(jnp.int32, (tiles + 1, 8, window), 1)
            none = jnp.zeros((1, 8, window), f32)
            for k in range(2):
                turned = pltpu.roll((gw[s, k] * scale).reshape(tiles, 8, window), lax.rem(row_s, 8), 1)
                wide = jnp.where(
                    sub17 >= row_s,
                    jnp.concatenate([turned, none], axis=0),
                    jnp.concatenate([none, turned], axis=0),
                )
                wide = pltpu.roll(wide, lax.rem(col_s, window), 2)
                shifted[s, k, 1:tiles + 2, 1] = jnp.where(lane17 >= col_s, wide, 0.0)
                shifted[s, k, 1:tiles + 2, 2] = jnp.where(lane17 < col_s, wide, 0.0)
            return 0

        lax.fori_loop(0, plan.slots, one, 0)

    def deposit(now, low, high):
        def lines(b, _):
            rows = [2 * b, 2 * b + 1]
            acc = [[[now[k, i, j] for j in range(plan.col_blocks)] for k in range(2)] for i in rows]
            for s in range(plan.slots):
                row0 = cut_of(s, s % cap)[0]
                at = [jnp.where((i >= row0) & (i <= row0 + tiles), i - row0 + 1, 0) for i in rows]
                for j in range(plan.col_blocks):
                    c = col_tab[s * plan.col_blocks + j]
                    for n in range(2):
                        for k in range(2):
                            acc[n][k][j] = acc[n][k][j] + shifted[s, k, at[n], c]
            for n, i in enumerate(rows):
                for k in range(2):
                    for j in range(plan.col_blocks):
                        next_spec[k, i, j] = acc[n][k][j]
            return 0

        lax.fori_loop(low // 2, high // 2, lines, 0)

    def light_one(it, d):
        n = plan.light
        return remote(
            light.at[pl.ds(flip(ty, d) * n, n)], lt_in.at[it, d], ls.at[it, d], lr.at[it, d], ty_dev[d]
        )

    def light_two(it, d):
        return remote(lx_in.at[it, 0], lx_in.at[it, d], xs.at[it, d], xr.at[it, d], tx_dev[d])

    def light_three(it, d):
        return remote(lm_in.at[it, 0], lm_in.at[it, d], ms.at[it, d], mr.at[it, d], ty_dev[d])

    def lighting(it, stage):
        if stage == 0:
            for d in range(1, nty):
                light_one(it, d).start()
        elif stage == 1:
            mine = light[pl.ds(ty * plan.light, plan.light)]
            for d in range(1, nty):
                light_one(it, d).wait()
                mine = mine + lt_in[it, d]
            lx_in[it, 0] = mine
            for d in range(1, plan.ntx):
                light_two(it, d).start()
        elif stage == 2:
            mine = lx_in[it, 0]
            for d in range(1, plan.ntx):
                light_two(it, d).wait()
                mine = mine + lx_in[it, d]
            lm_in[it, 0] = jnp.max(mine, axis=0)
            for d in range(1, nty):
                light_three(it, d).start()
        else:
            for d in range(1, nty):
                light_three(it, d).wait()

    def owned(at):
        return at * chunk // tiles, lax.rem(at * chunk, tiles)

    def step_a(it, g):
        return remote(
            grad.at[1 - core, pl.ds(g * per, per)], half_in.at[it, g], cs.at[it, g], cr.at[it, g], mate
        )

    def step_b(it, g, j):
        m, t = owned(chip_at[j])
        return remote(
            part.at[it, g, m, pl.ds(t, chunk)], rs_in.at[it, g, j], rs.at[it, g, j], rr.at[it, g, j], chip_dev[j]
        )

    def step_c(it, g, j):
        m, t = owned(chip)
        ref = probe.at[it + 1, core, g * per + m, pl.ds(t, chunk)]
        return remote(ref, ref, gs.at[it, g, j], gr.at[it, g, j], chip_dev[j])

    def step_d(it, g):
        ref = probe.at[it + 1, core, pl.ds(g * per, per)]
        return remote(ref, ref, bs.at[it, g], br.at[it, g], mate)

    def do_b(it, g):
        step_a(it, g).wait_recv()
        part[it, g] = grad[core, pl.ds(g * per, per)] + half_in[it, g]
        for j in range(len(chips)):
            step_b(it, g, j).start()

    def do_c(it, g, bottom):
        m, t = owned(chip)
        total = part[it, g, m, pl.ds(t, chunk)]
        for j in range(len(chips)):
            step_b(it, g, j).wait_recv()
            total = total + rs_in[it, g, j]
        at = g * per + m
        probe[it + 1, core, at, pl.ds(t, chunk)] = probe[it, core, at, pl.ds(t, chunk)] + total / bottom
        for j in range(len(chips)):
            step_c(it, g, j).start()

    def do_d(it, g):
        for j in range(len(chips)):
            step_c(it, g, j).wait_recv()
        step_d(it, g).start()

    def do_e(it, g):
        step_d(it, g).wait_recv()

    def close(it, g, _):
        step_a(it, g).wait_send()
        for j in range(len(chips)):
            step_b(it, g, j).wait_send()
            step_c(it, g, j).wait_send()
        step_d(it, g).wait_send()
        return 0

    windows(spec)
    lighting(0, 0)
    for it in range(ITERS):
        now = spec if it == 0 else next_spec

        def ahead(m, _):
            if it:
                g = m // per

                @pl.when(lax.rem(m, per) == 0)
                def _():
                    @pl.when(g + 1 < groups)
                    def _():
                        do_d(it - 1, g + 1)

                    do_e(it - 1, g)

            forward(it, m)
            return 0

        lax.fori_loop(0, modes, ahead, 0)
        if it:
            lighting(it, 1)
            lax.fori_loop(0, groups, functools.partial(close, it - 1), 0)

        def back(low, high, m, _):
            backward(it, m, low, high)
            g = m // per

            @pl.when(lax.rem(m, per) == per - 1)
            def _():
                step_a(it, g).start()

                @pl.when(g > 0)
                def _():
                    do_b(it, g - 1)

            @pl.when(m == modes // 2)
            def _():
                lighting(it, 2)

            return 0

        if it == 0:
            half = plan.units // 2
            factors(it, 0, half)

            def early(m, _):
                backward(it, m, 0, half)
                return 0

            lax.fori_loop(0, modes, early, 0)
            lighting(it, 1)
            factors(it, half, plan.units)
            lax.fori_loop(0, modes, functools.partial(back, half, plan.units), 0)
        else:
            factors(it, 0, plan.units)
            lax.fori_loop(0, modes, functools.partial(back, 0, plan.units), 0)
        shift(scale_of(it))
        do_b(it, groups - 1)
        deposit(now, 0, plan.row_blocks // 4)
        lighting(it, 3)
        bottom = jnp.max(jnp.max(lm_in[it], axis=0), keepdims=True) + SMALL_EPS
        for g in range(groups):
            if g == groups // 2:
                deposit(now, plan.row_blocks // 4, plan.row_blocks // 2)
            do_c(it, g, bottom)
        deposit(now, plan.row_blocks // 2, plan.row_blocks)
        if it + 1 < ITERS:
            windows(next_spec)
            lighting(it + 1, 0)
            do_d(it, 0)
    it = ITERS - 1
    store = [
        pltpu.make_async_copy(
            next_spec.at[:, :, j], spec_out.at[:, :, :, pl.ds(j * window, window)], out_sem.at[2 + j]
        )
        for j in range(plan.col_blocks)
    ]
    for copy in store:
        copy.start()
    for g in range(groups):
        do_d(it, g)
    for copy in pats:
        copy.wait_send()
    for g in range(groups):
        do_e(it, g)
    final = [
        pltpu.make_async_copy(probe.at[ITERS, k], probe_out.at[:, k], out_sem.at[k]) for k in range(2)
    ]
    for copy in final:
        copy.start()
    lax.fori_loop(0, groups, functools.partial(close, it), 0)
    for copy in store + final:
        copy.wait()


def hand_over_kernel(spec_in, probe_in, spec_out, probe_out, spec, probe, sems):
    lines = spec_in.shape[1] // PARTS
    copies = []
    for k in range(2):
        for n in range(PARTS):
            at = pl.ds(n * lines, lines)
            copies.append((spec_in.at[k, at], spec.at[k, at], spec_out.at[k, at]))
    for m in range(probe_in.shape[0]):
        copies.append((probe_in.at[m], probe.at[m], probe_out.at[m]))
    inward = [pltpu.make_async_copy(a, b, sems.at[0, n]) for n, (a, b, _) in enumerate(copies)]
    outward = [pltpu.make_async_copy(b, c, sems.at[1, n]) for n, (_, b, c) in enumerate(copies)]
    for copy in inward:
        copy.start()
    for first, second in zip(inward, outward):
        first.wait()
        second.start()
    for copy in outward:
        copy.wait()


def shards(specimen, probe_modes, patterns, tile_row, row_offset, col_offset):
    own, window, _ = patterns.shape
    modes = probe_modes.shape[0]
    nty, ntx = lax.axis_size("ty"), lax.axis_size("tx")
    plan = Plan(nty, ntx, own, window, modes, specimen.shape[1], specimen.shape[2])
    lefts, rights = dft_tables(window)
    f32, dma = jnp.float32, pltpu.SemaphoreType.DMA
    shape = specimen.shape
    view = (2, plan.row_blocks, 8, shape[2])
    spec_view = (2, plan.row_blocks, plan.col_blocks, 8, window)
    tiles, cap, groups, others = plan.tiles, plan.cap, plan.groups, plan.chips - 1
    plane = (tiles, 8, window)
    probe_view = (modes, 2) + plane
    both = lambda *n: dma((ITERS,) + n)
    scratch = [
        VMEM(patterns.shape, f32),
        VMEM(spec_view, f32),
        VMEM(spec_view, f32),
        VMEM(lefts.shape, jnp.bfloat16),
        VMEM(rights.shape, jnp.bfloat16),
        VMEM((ITERS + 1, 2, modes) + plane, f32),
        VMEM((2, modes) + plane, f32),
        VMEM(plane, f32),
        VMEM((plan.slots, 2, tiles + 2, 3, 8, window), f32),
        VMEM((nty, cap, window, window), f32),
        VMEM((nty, cap, window, window), f32),
        VMEM((nty, 8, window), jnp.int32),
        VMEM((nty, 8, window), jnp.int32),
        SMEM((nty, 8, window), jnp.int32),
        SMEM((plan.slots * plan.col_blocks,), jnp.int32),
        VMEM((plan.slots, 2, window, window), f32),
        VMEM((modes, plan.units, 2 * window, 2 * window), f32),
        VMEM((plan.units, window, 2 * window), f32),
        VMEM((plan.slots, 2, window, window), f32),
        VMEM((ITERS, groups, plan.per) + plane, f32),
        VMEM((ITERS, groups, plan.per) + plane, f32),
        VMEM((ITERS, groups, others, plan.chunk, 8, window), f32),
        VMEM((ITERS, nty, plan.light, 8, window), f32),
        VMEM((ITERS, ntx, plan.light, 8, window), f32),
        VMEM((ITERS, nty, 8, window), f32),
        dma((5 + plan.col_blocks,)), dma((1,)), dma((2 + plan.col_blocks,)),
        dma((nty,)), dma((nty,)), dma((nty,)), dma((nty,)),
        both(nty), both(nty), both(ntx), both(ntx), both(nty), both(nty),
        both(groups), both(groups), both(groups, others), both(groups, others),
        both(groups, others), both(groups, others), both(groups), both(groups),
    ]
    out, probe = pl.pallas_call(
        functools.partial(program_kernel, plan),
        out_shape=(jax.ShapeDtypeStruct(view, f32), jax.ShapeDtypeStruct(probe_view, f32)),
        in_specs=[pl.BlockSpec(memory_space=SMEM)] * 3 + [pl.BlockSpec(memory_space=pl.ANY)] * 5,
        out_specs=(pl.BlockSpec(memory_space=pl.ANY),) * 2,
        scratch_shapes=scratch,
        compiler_params=pltpu.CompilerParams(
            collective_id=0, has_side_effects=True, vmem_limit_bytes=LIMIT
        ),
        name="program",
    )(
        tile_row, row_offset, col_offset, patterns, specimen.reshape(view),
        probe_modes.reshape(probe_view), jnp.asarray(lefts), jnp.asarray(rights),
    )
    out, probe = pl.pallas_call(
        hand_over_kernel,
        out_shape=(jax.ShapeDtypeStruct(view, f32), jax.ShapeDtypeStruct(probe_view, f32)),
        in_specs=[pl.BlockSpec(memory_space=pl.ANY)] * 2,
        out_specs=(pl.BlockSpec(memory_space=pl.ANY),) * 2,
        scratch_shapes=[VMEM(view, f32), VMEM(probe_view, f32), dma((2, 2 * PARTS + modes))],
        name="hand_over",
    )(out, probe)
    return out.reshape(shape), probe.reshape(probe_modes.shape)


def solution(mesh):
    placed = (
        P(None, "ty", "tx"),
        P(),
        P(("ty", "tx"), None, None),
        P(("ty", "tx")),
        P(("ty", "tx")),
        P(("ty", "tx")),
    )
    return jax.shard_map(
        shards, mesh=mesh, in_specs=placed, out_specs=(P(None, "ty", "tx"), P()), check_vma=False
    )
```

```python
import functools
import math

import jax
import jax.numpy as jnp
import ml_dtypes
import numpy as np
from jax import lax
from jax.experimental import pallas as pl
from jax.experimental.pallas import tpu as pltpu
from jax.sharding import PartitionSpec as P

ITERS = 2
AMP_FLOOR = 0.3
OBJ_STEP = 1.0
SMALL_EPS = 1e-06
PARTS = 8

VMEM = pltpu.VMEM
SMEM = pltpu.SMEM
LIMIT = 60 * 1024 * 1024
MESH = pl.DeviceIdType.MESH


def dft_tables(length):
    counter = np.arange(length, dtype=np.int64)
    angles = (counter[:, None] * counter[None, :] % length) * (2.0 * math.pi / length)
    cos = np.cos(angles) / math.sqrt(length)
    sin = np.sin(angles) / math.sqrt(length)
    one = np.block([[cos, sin], [-sin, cos]])

    def parts(table):
        high = table.astype(ml_dtypes.bfloat16)
        return high, (table - high.astype(np.float64)).astype(ml_dtypes.bfloat16)

    lefts, rights = [], []
    for table in (one, one.T):
        high, low = parts(table)
        lefts.append(np.concatenate([high, low, high], axis=1))
        high, low = parts(table.T)
        rights.append(np.concatenate([high, high, low], axis=0))
    return np.stack(lefts), np.stack(rights)


def split(values):
    high = values.astype(jnp.bfloat16)
    low = (values - high.astype(jnp.float32)).astype(jnp.bfloat16)
    return high, low


def dot(a, b):
    return jnp.dot(a, b, preferred_element_type=jnp.float32)


def left(table, values):
    high, low = split(values)
    return dot(table, jnp.concatenate([high, high, low], axis=0))


def right(values, table):
    high, low = split(values)
    return dot(jnp.concatenate([high, low, high], axis=1), table)


def blocks2(a, b, c, d):
    return jnp.concatenate(
        [jnp.concatenate([a, b], axis=1), jnp.concatenate([c, d], axis=1)], axis=0
    )


def flip(index, mask):
    out, bit = index, 1
    while bit <= mask:
        if mask & bit:
            out = out + bit * (1 - 2 * lax.rem(index // bit, 2))
        bit *= 2
    return out


class Plan:
    def __init__(self, nty, ntx, own, window, modes, rows, cols):
        self.nty, self.ntx, self.ny = nty, ntx, ntx // 2
        self.own, self.window, self.modes = own, window, modes
        self.cap = max(2, 2 * own // nty)
        self.slots = nty * self.cap
        self.units = self.slots // 2
        self.batch = self.units // 2
        while self.batch > 4:
            self.batch //= 2
        self.wide = 2 * self.batch
        self.tiles = window // 8
        self.row_blocks, self.col_blocks = rows // 8, cols // window
        self.chips = nty * self.ny
        self.groups = max(1, min(modes, modes * self.tiles // self.chips))
        self.per = modes // self.groups
        self.chunk = self.per * self.tiles // self.chips
        self.light = self.tiles // nty


def program_kernel(
    plan,
    tile_ref, row_ref, col_ref, pat_any, spec_any, probe_any, left_any, right_any,
    spec_out, probe_out,
    pat, spec, next_spec, left_t, right_t, probe, grad, light, shifted,
    send_pat, got_pat, send_head, got_head, head, col_tab, wave_w, far, power_ref, gw,
    half_in, part, rs_in, lt_in, lx_in, lm_in,
    load_sem, head_sem, out_sem,
    hs, hr, ps, pr, ls, lr, xs, xr, ms, mr, cs, cr, rs, rr, gs, gr, bs, br,
):
    f32 = jnp.float32
    nty, ny, cap, window, modes = plan.nty, plan.ny, plan.cap, plan.window, plan.modes
    tiles, chunk, groups, per = plan.tiles, plan.chunk, plan.groups, plan.per
    ty, tx = lax.axis_index("ty"), lax.axis_index("tx")
    core, y = lax.rem(tx, 2), tx // 2
    ty_dev = {d: {"ty": flip(ty, d)} for d in range(1, nty)}
    tx_dev = {d: {"tx": flip(tx, d)} for d in range(1, plan.ntx)}
    mate = tx_dev[1]
    near_first = list(range(1, nty))
    chips = [(a, e) for a in range(nty - 1, -1, -1) for e in range(ny - 1, -1, -1) if a or e]
    chip_dev = [{"ty": flip(ty, a), "tx": flip(tx, 2 * e)} for a, e in chips]
    chip_at = [flip(y, e) * nty + flip(ty, a) for a, e in chips]
    chip = y * nty + ty

    barrier = pltpu.get_barrier_semaphore()
    others = list(tx_dev.values()) + list(ty_dev.values())
    others += [dev for (a, e), dev in zip(chips, chip_dev) if a and e]
    for device in others:
        pl.semaphore_signal(barrier, inc=1, device_id=device, device_id_type=MESH)

    loads = [
        pltpu.make_async_copy(src, dst, load_sem.at[k])
        for k, (src, dst) in enumerate((
            (pat_any, pat), (probe_any.at[:, 0], probe.at[0, 0]), (probe_any.at[:, 1], probe.at[0, 1]),
            (left_any, left_t), (right_any, right_t),
        ))
    ] + [
        pltpu.make_async_copy(
            spec_any.at[:, :, :, pl.ds(j * window, window)], spec.at[:, :, j], load_sem.at[5 + j]
        )
        for j in range(plan.col_blocks)
    ]
    for copy in loads:
        copy.start()

    sent = []

    def remote(src, dst, s, r, device):
        return pltpu.make_async_remote_copy(
            src_ref=src, dst_ref=dst, send_sem=s, recv_sem=r, device_id=device, device_id_type=MESH
        )

    lane = lax.broadcasted_iota(jnp.int32, (8, window), 1)
    picks = {}
    for d in range(nty):
        tile = flip(ty, d)
        seen = jnp.int32(0)
        place = [jnp.int32(0)] * cap
        valid = [jnp.int32(0)] * cap
        for p in range(plan.own):
            hit = (tile_ref[p] == tile).astype(jnp.int32)
            for r in range(cap):
                take = hit * (seen == r).astype(jnp.int32)
                place[r] = place[r] + take * p
                valid[r] = valid[r] + take
            seen = seen + hit
        vector = jnp.zeros((8, window), jnp.int32)
        for r in range(cap):
            for k, value in enumerate((row_ref[place[r]], col_ref[place[r]], valid[r])):
                vector = jnp.where(lane == 3 * r + k, value, vector)
        if d == 0:
            got_head[0] = vector
        else:
            send_head[d] = vector
        picks[d] = place

    loads[0].wait()
    for d in [0] + near_first:
        for r in range(cap):
            root = jnp.sqrt(pat[picks[d][r]])
            if d == 0:
                got_pat[0, r] = root
            else:
                send_pat[d, r] = root

    pl.semaphore_wait(barrier, len(others))
    heads = [
        remote(send_head.at[d], got_head.at[d], hs.at[d], hr.at[d], ty_dev[d]) for d in near_first
    ]
    pats = [
        remote(send_pat.at[d], got_pat.at[d], ps.at[d], pr.at[d], ty_dev[d]) for d in near_first
    ]
    for copy in heads + pats:
        copy.start()
    shifted[...] = jnp.zeros_like(shifted)
    for copy in loads[1:]:
        copy.wait()
    for copy in heads:
        copy.wait()
    to_scalar = pltpu.make_async_copy(got_head, head, head_sem.at[0])
    to_scalar.start()
    to_scalar.wait()

    def cut_of(s, r):
        row, col = head[s // cap, 0, 3 * r], head[s // cap, 0, 3 * r + 1]
        row0 = jnp.minimum(row // 8, plan.row_blocks - tiles - 1)
        col0 = jnp.minimum(col // window, plan.col_blocks - 2)
        return row0, col0, row - row0 * 8, col - col0 * window

    def tab(s, _):
        _, col0, _, _ = cut_of(s, lax.rem(s, cap))
        for j in range(plan.col_blocks):
            col_tab[s * plan.col_blocks + j] = jnp.where((j >= col0) & (j <= col0 + 1), j - col0 + 1, 0)
        return 0

    lax.fori_loop(0, plan.slots, tab, 0)

    def windows(now):
        light[...] = jnp.zeros_like(light)

        def cut(s, _):
            r = lax.rem(s, cap)
            row0, col0, row_s, col_s = cut_of(s, r)
            valid = head[s // cap, 0, 3 * r + 2].astype(f32)
            sub8 = lax.broadcasted_iota(jnp.int32, (tiles, 8, window), 1)
            lane17 = lax.broadcasted_iota(jnp.int32, (tiles + 1, 8, window), 2)
            bright = jnp.zeros((tiles, 8, window), f32)
            for k in range(2):
                first = jnp.stack([now[k, row0 + a, col0] for a in range(tiles + 1)])
                second = jnp.stack([now[k, row0 + a, col0 + 1] for a in range(tiles + 1)])
                joined = jnp.where(lane17 < col_s, second, first)
                joined = pltpu.roll(joined, lax.rem(window - col_s, window), 2)
                turned = pltpu.roll(joined, lax.rem(8 - row_s, 8), 1)
                picked = jnp.where(sub8 < 8 - row_s, turned[:tiles], turned[1:]) * valid
                wave_w[s, k] = picked.reshape(window, window)
                bright = bright + picked * picked
            light[...] += bright
            return 0

        lax.fori_loop(0, plan.slots, cut, 0, unroll=4)

    def scale_of(it):
        total = jnp.zeros((tiles, 8, window), f32)
        for m in range(modes):
            total = total + (probe[it, 0, m] ** 2 + probe[it, 1, m] ** 2)
        return OBJ_STEP / (jnp.max(total.reshape(window, window), keepdims=True) + SMALL_EPS)

    def planes(it, m):
        return [probe[it, k, m].reshape(window, window) for k in range(2)]

    def turn(mids):
        rows = [
            jnp.concatenate([mid[half * window:(half + 1) * window, part * window:(part + 1) * window]
                             for half in range(2)], axis=1)
            for mid in mids for part in range(2)
        ]
        return rows

    def forward(it, m):
        p_re, p_im = planes(it, m)

        def some(b, _):
            for v in range(plan.wide):
                u = b * plan.wide + v
                waves = []
                for r in range(2):
                    w_re, w_im = wave_w[2 * u + r, 0], wave_w[2 * u + r, 1]
                    waves.append(jnp.concatenate(
                        [p_re * w_re - p_im * w_im, p_re * w_im + p_im * w_re], axis=1
                    ))
                mid = right(jnp.concatenate(waves, axis=0), right_t[0])
                spread = left(left_t[0], jnp.concatenate(turn([mid]), axis=0))
                far[m, u] = spread
                square = spread[:window] ** 2 + spread[window:] ** 2
                power_ref[u] = jnp.where(m == 0, square, power_ref[u] + square)
            return 0

        lax.fori_loop(0, plan.units // plan.wide, some, 0)

    def factors(it, low, high):
        def one(u, _):
            if it == 0:
                @pl.when(lax.rem(2 * u, cap) == 0)
                def _():
                    d = 2 * u // cap

                    @pl.when(d > 0)
                    def _():
                        remote(send_pat.at[d], got_pat.at[d], ps.at[d], pr.at[d], ty_dev[1]).wait_recv()
            d, r = 2 * u // cap, lax.rem(2 * u, cap)
            root = jnp.concatenate([got_pat[d, r], got_pat[d, r + 1]], axis=1)
            power_ref[u] = root / jnp.maximum(jnp.sqrt(power_ref[u]), AMP_FLOOR) - 1.0
            return 0

        lax.fori_loop(low, high, one, 0, unroll=2)

    def backward(it, m, low, high):
        p_re, p_im = planes(it, m)
        batch = plan.batch if it == 0 else plan.wide

        def some(b, _):
            add_re = jnp.zeros((window, window), f32)
            add_im = jnp.zeros((window, window), f32)
            for v in range(batch):
                u = b * batch + v
                factor = power_ref[u]
                mid = left(left_t[1], far[m, u] * jnp.concatenate([factor, factor], axis=0))
                back = right(jnp.concatenate(turn([mid]), axis=0), right_t[1])
                for r in range(2):
                    w_re, w_im = wave_w[2 * u + r, 0], wave_w[2 * u + r, 1]
                    line = slice(r * window, (r + 1) * window)
                    b_re, b_im = back[line, :window], back[line, window:]
                    add_re = add_re + (w_re * b_re + w_im * b_im)
                    add_im = add_im + (w_re * b_im - w_im * b_re)
                    g_re = p_re * b_re + p_im * b_im
                    g_im = p_re * b_im - p_im * b_re
                    gw[2 * u + r, 0] = jnp.where(m == 0, g_re, gw[2 * u + r, 0] + g_re)
                    gw[2 * u + r, 1] = jnp.where(m == 0, g_im, gw[2 * u + r, 1] + g_im)
            for k, add in enumerate((add_re, add_im)):
                add = add.reshape(tiles, 8, window)
                grad[k, m] = jnp.where(b == 0, add, grad[k, m] + add)
            return 0

        lax.fori_loop(low // batch, high // batch, some, 0)

    def shift(scale, low, high):
        def one(s, _):
            _, _, row_s, col_s = cut_of(s, lax.rem(s, cap))
            lane17 = lax.broadcasted_iota(jnp.int32, (tiles + 1, 8, window), 2)
            sub17 = lax.broadcasted_iota(jnp.int32, (tiles + 1, 8, window), 1)
            none = jnp.zeros((1, 8, window), f32)
            for k in range(2):
                turned = pltpu.roll((gw[s, k] * scale).reshape(tiles, 8, window), lax.rem(row_s, 8), 1)
                wide = jnp.where(
                    sub17 >= row_s,
                    jnp.concatenate([turned, none], axis=0),
                    jnp.concatenate([none, turned], axis=0),
                )
                wide = pltpu.roll(wide, lax.rem(col_s, window), 2)
                shifted[s, k, 1:tiles + 2, 1] = jnp.where(lane17 >= col_s, wide, 0.0)
                shifted[s, k, 1:tiles + 2, 2] = jnp.where(lane17 < col_s, wide, 0.0)
            return 0

        lax.fori_loop(low, high, one, 0, unroll=4)

    def deposit(now, low, high):
        def lines(b, _):
            rows = [2 * b, 2 * b + 1]
            acc = [[[now[k, i, j] for j in range(plan.col_blocks)] for k in range(2)] for i in rows]
            for s in range(plan.slots):
                row0 = cut_of(s, s % cap)[0]
                at = [jnp.where((i >= row0) & (i <= row0 + tiles), i - row0 + 1, 0) for i in rows]
                for j in range(plan.col_blocks):
                    c = col_tab[s * plan.col_blocks + j]
                    for n in range(2):
                        for k in range(2):
                            acc[n][k][j] = acc[n][k][j] + shifted[s, k, at[n], c]
            for n, i in enumerate(rows):
                for k in range(2):
                    for j in range(plan.col_blocks):
                        next_spec[k, i, j] = acc[n][k][j]
            return 0

        lax.fori_loop(low // 2, high // 2, lines, 0)

    def light_one(it, d):
        n = plan.light
        return remote(
            light.at[pl.ds(flip(ty, d) * n, n)], lt_in.at[it, d], ls.at[it, d], lr.at[it, d], ty_dev[d]
        )

    def light_two(it, d):
        return remote(lx_in.at[it, 0], lx_in.at[it, d], xs.at[it, d], xr.at[it, d], tx_dev[d])

    def light_three(it, d):
        return remote(lm_in.at[it, 0], lm_in.at[it, d], ms.at[it, d], mr.at[it, d], ty_dev[d])

    def lighting(it, stage):
        if stage == 0:
            for d in range(1, nty):
                light_one(it, d).start()
        elif stage == 1:
            mine = light[pl.ds(ty * plan.light, plan.light)]
            for d in range(1, nty):
                light_one(it, d).wait()
                mine = mine + lt_in[it, d]
            lx_in[it, 0] = mine
            for d in range(1, plan.ntx):
                light_two(it, d).start()
        elif stage == 2:
            mine = lx_in[it, 0]
            for d in range(1, plan.ntx):
                light_two(it, d).wait()
                mine = mine + lx_in[it, d]
            lm_in[it, 0] = jnp.max(mine, axis=0)
            for d in range(1, nty):
                light_three(it, d).start()
        else:
            for d in range(1, nty):
                light_three(it, d).wait()

    def owned(at):
        return at * chunk // tiles, lax.rem(at * chunk, tiles)

    def step_a(it, g):
        return remote(
            grad.at[1 - core, pl.ds(g * per, per)], half_in.at[it, g], cs.at[it, g], cr.at[it, g], mate
        )

    def step_b(it, g, j):
        m, t = owned(chip_at[j])
        return remote(
            part.at[it, g, m, pl.ds(t, chunk)], rs_in.at[it, g, j], rs.at[it, g, j], rr.at[it, g, j], chip_dev[j]
        )

    def step_c(it, g, j):
        m, t = owned(chip)
        ref = probe.at[it + 1, core, g * per + m, pl.ds(t, chunk)]
        return remote(ref, ref, gs.at[it, g, j], gr.at[it, g, j], chip_dev[j])

    def step_d(it, g):
        ref = probe.at[it + 1, core, pl.ds(g * per, per)]
        return remote(ref, ref, bs.at[it, g], br.at[it, g], mate)

    def do_b(it, g):
        step_a(it, g).wait_recv()
        part[it, g] = grad[core, pl.ds(g * per, per)] + half_in[it, g]
        for j in range(len(chips)):
            step_b(it, g, j).start()

    def do_c(it, g, bottom):
        m, t = owned(chip)
        total = part[it, g, m, pl.ds(t, chunk)]
        for j in range(len(chips)):
            step_b(it, g, j).wait_recv()
            total = total + rs_in[it, g, j]
        at = g * per + m
        probe[it + 1, core, at, pl.ds(t, chunk)] = probe[it, core, at, pl.ds(t, chunk)] + total / bottom
        for j in range(len(chips)):
            step_c(it, g, j).start()

    def do_d(it, g):
        for j in range(len(chips)):
            step_c(it, g, j).wait_recv()
        step_d(it, g).start()

    def do_e(it, g):
        step_d(it, g).wait_recv()

    def close(it, g, _):
        step_a(it, g).wait_send()
        for j in range(len(chips)):
            step_b(it, g, j).wait_send()
            step_c(it, g, j).wait_send()
        step_d(it, g).wait_send()
        return 0

    windows(spec)
    lighting(0, 0)
    for it in range(ITERS):
        now = spec if it == 0 else next_spec

        def ahead(m, _):
            if it:
                g = m // per

                @pl.when(lax.rem(m, per) == 0)
                def _():
                    @pl.when(g + 1 < groups)
                    def _():
                        do_d(it - 1, g + 1)

                    do_e(it - 1, g)

            forward(it, m)
            return 0

        lax.fori_loop(0, modes, ahead, 0)
        if it:
            lighting(it, 1)
            lax.fori_loop(0, groups, functools.partial(close, it - 1), 0)

        def back(low, high, m, _):
            backward(it, m, low, high)
            g = m // per

            @pl.when(lax.rem(m, per) == per - 1)
            def _():
                step_a(it, g).start()

                @pl.when(g > 0)
                def _():
                    do_b(it, g - 1)

            @pl.when(m == modes // 2)
            def _():
                lighting(it, 2)

            return 0

        if it == 0:
            half = plan.units // 2
            factors(it, 0, half)

            def early(m, _):
                backward(it, m, 0, half)
                return 0

            lax.fori_loop(0, modes, early, 0)
            lighting(it, 1)
            factors(it, half, plan.units)
            lax.fori_loop(0, modes, functools.partial(back, half, plan.units), 0)
        else:
            factors(it, 0, plan.units)
            lax.fori_loop(0, modes, functools.partial(back, 0, plan.units), 0)
        scale = scale_of(it)
        shift(scale, 0, plan.slots // 2)
        do_b(it, groups - 1)
        shift(scale, plan.slots // 2, plan.slots)
        deposit(now, 0, plan.row_blocks // 4)
        lighting(it, 3)
        bottom = jnp.max(jnp.max(lm_in[it], axis=0), keepdims=True) + SMALL_EPS
        for g in range(groups):
            if g == groups // 2:
                deposit(now, plan.row_blocks // 4, plan.row_blocks // 2)
            do_c(it, g, bottom)
        deposit(now, plan.row_blocks // 2, plan.row_blocks)
        if it + 1 < ITERS:
            windows(next_spec)
            lighting(it + 1, 0)
            do_d(it, 0)
    it = ITERS - 1
    store = [
        pltpu.make_async_copy(
            next_spec.at[:, :, j], spec_out.at[:, :, :, pl.ds(j * window, window)], out_sem.at[2 + j]
        )
        for j in range(plan.col_blocks)
    ]
    for copy in store:
        copy.start()
    for g in range(groups):
        do_d(it, g)
    for copy in pats:
        copy.wait_send()
    for g in range(groups):
        do_e(it, g)
    final = [
        pltpu.make_async_copy(probe.at[ITERS, k], probe_out.at[:, k], out_sem.at[k]) for k in range(2)
    ]
    for copy in final:
        copy.start()
    lax.fori_loop(0, groups, functools.partial(close, it), 0)
    for copy in store + final:
        copy.wait()


def hand_over_kernel(spec_in, probe_in, spec_out, probe_out, spec, probe, sems):
    lines = spec_in.shape[1] // PARTS
    copies = []
    for k in range(2):
        for n in range(PARTS):
            at = pl.ds(n * lines, lines)
            copies.append((spec_in.at[k, at], spec.at[k, at], spec_out.at[k, at]))
    for m in range(probe_in.shape[0]):
        copies.append((probe_in.at[m], probe.at[m], probe_out.at[m]))
    inward = [pltpu.make_async_copy(a, b, sems.at[0, n]) for n, (a, b, _) in enumerate(copies)]
    outward = [pltpu.make_async_copy(b, c, sems.at[1, n]) for n, (_, b, c) in enumerate(copies)]
    for copy in inward:
        copy.start()
    for first, second in zip(inward, outward):
        first.wait()
        second.start()
    for copy in outward:
        copy.wait()


def shards(specimen, probe_modes, patterns, tile_row, row_offset, col_offset):
    own, window, _ = patterns.shape
    modes = probe_modes.shape[0]
    nty, ntx = lax.axis_size("ty"), lax.axis_size("tx")
    plan = Plan(nty, ntx, own, window, modes, specimen.shape[1], specimen.shape[2])
    lefts, rights = dft_tables(window)
    f32, dma = jnp.float32, pltpu.SemaphoreType.DMA
    shape = specimen.shape
    view = (2, plan.row_blocks, 8, shape[2])
    spec_view = (2, plan.row_blocks, plan.col_blocks, 8, window)
    tiles, cap, groups, others = plan.tiles, plan.cap, plan.groups, plan.chips - 1
    plane = (tiles, 8, window)
    probe_view = (modes, 2) + plane
    both = lambda *n: dma((ITERS,) + n)
    scratch = [
        VMEM(patterns.shape, f32),
        VMEM(spec_view, f32),
        VMEM(spec_view, f32),
        VMEM(lefts.shape, jnp.bfloat16),
        VMEM(rights.shape, jnp.bfloat16),
        VMEM((ITERS + 1, 2, modes) + plane, f32),
        VMEM((2, modes) + plane, f32),
        VMEM(plane, f32),
        VMEM((plan.slots, 2, tiles + 2, 3, 8, window), f32),
        VMEM((nty, cap, window, window), f32),
        VMEM((nty, cap, window, window), f32),
        VMEM((nty, 8, window), jnp.int32),
        VMEM((nty, 8, window), jnp.int32),
        SMEM((nty, 8, window), jnp.int32),
        SMEM((plan.slots * plan.col_blocks,), jnp.int32),
        VMEM((plan.slots, 2, window, window), f32),
        VMEM((modes, plan.units, 2 * window, 2 * window), f32),
        VMEM((plan.units, window, 2 * window), f32),
        VMEM((plan.slots, 2, window, window), f32),
        VMEM((ITERS, groups, plan.per) + plane, f32),
        VMEM((ITERS, groups, plan.per) + plane, f32),
        VMEM((ITERS, groups, others, plan.chunk, 8, window), f32),
        VMEM((ITERS, nty, plan.light, 8, window), f32),
        VMEM((ITERS, ntx, plan.light, 8, window), f32),
        VMEM((ITERS, nty, 8, window), f32),
        dma((5 + plan.col_blocks,)), dma((1,)), dma((2 + plan.col_blocks,)),
        dma((nty,)), dma((nty,)), dma((nty,)), dma((nty,)),
        both(nty), both(nty), both(ntx), both(ntx), both(nty), both(nty),
        both(groups), both(groups), both(groups, others), both(groups, others),
        both(groups, others), both(groups, others), both(groups), both(groups),
    ]
    out, probe = pl.pallas_call(
        functools.partial(program_kernel, plan),
        out_shape=(jax.ShapeDtypeStruct(view, f32), jax.ShapeDtypeStruct(probe_view, f32)),
        in_specs=[pl.BlockSpec(memory_space=SMEM)] * 3 + [pl.BlockSpec(memory_space=pl.ANY)] * 5,
        out_specs=(pl.BlockSpec(memory_space=pl.ANY),) * 2,
        scratch_shapes=scratch,
        compiler_params=pltpu.CompilerParams(
            collective_id=0, has_side_effects=True, vmem_limit_bytes=LIMIT
        ),
        name="program",
    )(
        tile_row, row_offset, col_offset, patterns, specimen.reshape(view),
        probe_modes.reshape(probe_view), jnp.asarray(lefts), jnp.asarray(rights),
    )
    out, probe = pl.pallas_call(
        hand_over_kernel,
        out_shape=(jax.ShapeDtypeStruct(view, f32), jax.ShapeDtypeStruct(probe_view, f32)),
        in_specs=[pl.BlockSpec(memory_space=pl.ANY)] * 2,
        out_specs=(pl.BlockSpec(memory_space=pl.ANY),) * 2,
        scratch_shapes=[VMEM(view, f32), VMEM(probe_view, f32), dma((2, 2 * PARTS + modes))],
        name="hand_over",
    )(out, probe)
    return out.reshape(shape), probe.reshape(probe_modes.shape)


def solution(mesh):
    placed = (
        P(None, "ty", "tx"),
        P(),
        P(("ty", "tx"), None, None),
        P(("ty", "tx")),
        P(("ty", "tx")),
        P(("ty", "tx")),
    )
    return jax.shard_map(
        shards, mesh=mesh, in_specs=placed, out_specs=(P(None, "ty", "tx"), P()), check_vma=False
    )
```

```python
import functools
import math

import jax
import jax.numpy as jnp
import ml_dtypes
import numpy as np
from jax import lax
from jax.experimental import pallas as pl
from jax.experimental.pallas import tpu as pltpu
from jax.sharding import PartitionSpec as P

ITERS = 2
AMP_FLOOR = 0.3
OBJ_STEP = 1.0
SMALL_EPS = 1e-06
PARTS = 4

VMEM = pltpu.VMEM
SMEM = pltpu.SMEM
LIMIT = 60 * 1024 * 1024
MESH = pl.DeviceIdType.MESH


def dft_tables(length):
    counter = np.arange(length, dtype=np.int64)
    angles = (counter[:, None] * counter[None, :] % length) * (2.0 * math.pi / length)
    cos = np.cos(angles) / math.sqrt(length)
    sin = np.sin(angles) / math.sqrt(length)
    one = np.block([[cos, sin], [-sin, cos]])

    def parts(table):
        high = table.astype(ml_dtypes.bfloat16)
        return high, (table - high.astype(np.float64)).astype(ml_dtypes.bfloat16)

    lefts, rights = [], []
    for table in (one, one.T):
        high, low = parts(table)
        lefts.append(np.concatenate([high, low, high], axis=1))
        high, low = parts(table.T)
        rights.append(np.concatenate([high, high, low], axis=0))
    return np.stack(lefts), np.stack(rights)


def split(values):
    high = values.astype(jnp.bfloat16)
    low = (values - high.astype(jnp.float32)).astype(jnp.bfloat16)
    return high, low


def dot(a, b):
    return jnp.dot(a, b, preferred_element_type=jnp.float32)


def left(table, values):
    high, low = split(values)
    return dot(table, jnp.concatenate([high, high, low], axis=0))


def right(values, table):
    high, low = split(values)
    return dot(jnp.concatenate([high, low, high], axis=1), table)


def blocks2(a, b, c, d):
    return jnp.concatenate(
        [jnp.concatenate([a, b], axis=1), jnp.concatenate([c, d], axis=1)], axis=0
    )


def flip(index, mask):
    out, bit = index, 1
    while bit <= mask:
        if mask & bit:
            out = out + bit * (1 - 2 * lax.rem(index // bit, 2))
        bit *= 2
    return out


class Plan:
    def __init__(self, nty, ntx, own, window, modes, rows, cols):
        self.nty, self.ntx, self.ny = nty, ntx, ntx // 2
        self.own, self.window, self.modes = own, window, modes
        self.cap = max(2, 2 * own // nty)
        self.slots = nty * self.cap
        self.units = self.slots // 2
        self.batch = self.units // 2
        while self.batch > 4:
            self.batch //= 2
        self.wide = 2 * self.batch
        self.tiles = window // 8
        self.row_blocks, self.col_blocks = rows // 8, cols // window
        self.chips = nty * self.ny
        self.groups = max(1, min(modes, modes * self.tiles // self.chips))
        self.per = modes // self.groups
        self.chunk = self.per * self.tiles // self.chips
        self.light = self.tiles // nty


def program_kernel(
    plan,
    tile_ref, row_ref, col_ref, pat_any, spec_any, probe_any, left_any, right_any,
    spec_out, probe_out,
    pat, spec, next_spec, left_t, right_t, probe, grad, light, shifted,
    send_pat, got_pat, send_head, got_head, head, col_tab, wave_w, far, power_ref, gw,
    half_in, part, rs_in, lt_in, lx_in, lm_in,
    load_sem, head_sem, out_sem,
    hs, hr, ps, pr, ls, lr, xs, xr, ms, mr, cs, cr, rs, rr, gs, gr, bs, br,
):
    f32 = jnp.float32
    nty, ny, cap, window, modes = plan.nty, plan.ny, plan.cap, plan.window, plan.modes
    tiles, chunk, groups, per = plan.tiles, plan.chunk, plan.groups, plan.per
    ty, tx = lax.axis_index("ty"), lax.axis_index("tx")
    core, y = lax.rem(tx, 2), tx // 2
    ty_dev = {d: {"ty": flip(ty, d)} for d in range(1, nty)}
    tx_dev = {d: {"tx": flip(tx, d)} for d in range(1, plan.ntx)}
    mate = tx_dev[1]
    near_first = list(range(1, nty))
    chips = [(a, e) for a in range(nty - 1, -1, -1) for e in range(ny - 1, -1, -1) if a or e]
    chip_dev = [{"ty": flip(ty, a), "tx": flip(tx, 2 * e)} for a, e in chips]
    chip_at = [flip(y, e) * nty + flip(ty, a) for a, e in chips]
    chip = y * nty + ty

    barrier = pltpu.get_barrier_semaphore()
    others = list(tx_dev.values()) + list(ty_dev.values())
    others += [dev for (a, e), dev in zip(chips, chip_dev) if a and e]
    for device in others:
        pl.semaphore_signal(barrier, inc=1, device_id=device, device_id_type=MESH)

    loads = [
        pltpu.make_async_copy(src, dst, load_sem.at[k])
        for k, (src, dst) in enumerate((
            (pat_any, pat), (probe_any.at[:, 0], probe.at[0, 0]), (probe_any.at[:, 1], probe.at[0, 1]),
            (left_any, left_t), (right_any, right_t),
        ))
    ] + [
        pltpu.make_async_copy(
            spec_any.at[:, :, :, pl.ds(j * window, window)], spec.at[:, :, j], load_sem.at[5 + j]
        )
        for j in range(plan.col_blocks)
    ]
    for copy in loads:
        copy.start()

    sent = []

    def remote(src, dst, s, r, device):
        return pltpu.make_async_remote_copy(
            src_ref=src, dst_ref=dst, send_sem=s, recv_sem=r, device_id=device, device_id_type=MESH
        )

    lane = lax.broadcasted_iota(jnp.int32, (8, window), 1)
    picks = {}
    for d in range(nty):
        tile = flip(ty, d)
        seen = jnp.int32(0)
        place = [jnp.int32(0)] * cap
        valid = [jnp.int32(0)] * cap
        for p in range(plan.own):
            hit = (tile_ref[p] == tile).astype(jnp.int32)
            for r in range(cap):
                take = hit * (seen == r).astype(jnp.int32)
                place[r] = place[r] + take * p
                valid[r] = valid[r] + take
            seen = seen + hit
        vector = jnp.zeros((8, window), jnp.int32)
        for r in range(cap):
            for k, value in enumerate((row_ref[place[r]], col_ref[place[r]], valid[r])):
                vector = jnp.where(lane == 3 * r + k, value, vector)
        if d == 0:
            got_head[0] = vector
        else:
            send_head[d] = vector
        picks[d] = place

    loads[0].wait()
    for d in [0] + near_first:
        for r in range(cap):
            root = jnp.sqrt(pat[picks[d][r]])
            if d == 0:
                got_pat[0, r] = root
            else:
                send_pat[d, r] = root

    pl.semaphore_wait(barrier, len(others))
    heads = [
        remote(send_head.at[d], got_head.at[d], hs.at[d], hr.at[d], ty_dev[d]) for d in near_first
    ]
    pats = [
        remote(send_pat.at[d], got_pat.at[d], ps.at[d], pr.at[d], ty_dev[d]) for d in near_first
    ]
    for copy in heads + pats:
        copy.start()
    shifted[...] = jnp.zeros_like(shifted)
    for copy in loads[1:]:
        copy.wait()
    for copy in heads:
        copy.wait()
    to_scalar = pltpu.make_async_copy(got_head, head, head_sem.at[0])
    to_scalar.start()
    to_scalar.wait()

    def cut_of(s, r):
        row, col = head[s // cap, 0, 3 * r], head[s // cap, 0, 3 * r + 1]
        row0 = jnp.minimum(row // 8, plan.row_blocks - tiles - 1)
        col0 = jnp.minimum(col // window, plan.col_blocks - 2)
        return row0, col0, row - row0 * 8, col - col0 * window

    def tab(s, _):
        _, col0, _, _ = cut_of(s, lax.rem(s, cap))
        for j in range(plan.col_blocks):
            col_tab[s * plan.col_blocks + j] = jnp.where((j >= col0) & (j <= col0 + 1), j - col0 + 1, 0)
        return 0

    lax.fori_loop(0, plan.slots, tab, 0)

    def windows(now):
        light[...] = jnp.zeros_like(light)

        def cut(s, _):
            r = lax.rem(s, cap)
            row0, col0, row_s, col_s = cut_of(s, r)
            valid = head[s // cap, 0, 3 * r + 2].astype(f32)
            sub8 = lax.broadcasted_iota(jnp.int32, (tiles, 8, window), 1)
            lane17 = lax.broadcasted_iota(jnp.int32, (tiles + 1, 8, window), 2)
            bright = jnp.zeros((tiles, 8, window), f32)
            for k in range(2):
                first = jnp.stack([now[k, row0 + a, col0] for a in range(tiles + 1)])
                second = jnp.stack([now[k, row0 + a, col0 + 1] for a in range(tiles + 1)])
                joined = jnp.where(lane17 < col_s, second, first)
                joined = pltpu.roll(joined, lax.rem(window - col_s, window), 2)
                turned = pltpu.roll(joined, lax.rem(8 - row_s, 8), 1)
                picked = jnp.where(sub8 < 8 - row_s, turned[:tiles], turned[1:]) * valid
                wave_w[s, k] = picked.reshape(window, window)
                bright = bright + picked * picked
            light[...] += bright
            return 0

        lax.fori_loop(0, plan.slots, cut, 0, unroll=4)

    def scale_of(it):
        total = jnp.zeros((tiles, 8, window), f32)
        for m in range(modes):
            total = total + (probe[it, 0, m] ** 2 + probe[it, 1, m] ** 2)
        return OBJ_STEP / (jnp.max(total.reshape(window, window), keepdims=True) + SMALL_EPS)

    def planes(it, m):
        return [probe[it, k, m].reshape(window, window) for k in range(2)]

    def turn(mids):
        rows = [
            jnp.concatenate([mid[half * window:(half + 1) * window, part * window:(part + 1) * window]
                             for half in range(2)], axis=1)
            for mid in mids for part in range(2)
        ]
        return rows

    def forward(it, m):
        p_re, p_im = planes(it, m)

        def some(b, _):
            for v in range(plan.wide):
                u = b * plan.wide + v
                waves = []
                for r in range(2):
                    w_re, w_im = wave_w[2 * u + r, 0], wave_w[2 * u + r, 1]
                    waves.append(jnp.concatenate(
                        [p_re * w_re - p_im * w_im, p_re * w_im + p_im * w_re], axis=1
                    ))
                mid = right(jnp.concatenate(waves, axis=0), right_t[0])
                spread = left(left_t[0], jnp.concatenate(turn([mid]), axis=0))
                far[m, u] = spread
                square = spread[:window] ** 2 + spread[window:] ** 2
                power_ref[u] = jnp.where(m == 0, square, power_ref[u] + square)
            return 0

        lax.fori_loop(0, plan.units // plan.wide, some, 0)

    def factors(it, low, high):
        def one(u, _):
            if it == 0:
                @pl.when(lax.rem(2 * u, cap) == 0)
                def _():
                    d = 2 * u // cap

                    @pl.when(d > 0)
                    def _():
                        remote(send_pat.at[d], got_pat.at[d], ps.at[d], pr.at[d], ty_dev[1]).wait_recv()
            d, r = 2 * u // cap, lax.rem(2 * u, cap)
            root = jnp.concatenate([got_pat[d, r], got_pat[d, r + 1]], axis=1)
            power_ref[u] = root / jnp.maximum(jnp.sqrt(power_ref[u]), AMP_FLOOR) - 1.0
            return 0

        lax.fori_loop(low, high, one, 0, unroll=2)

    def backward(it, m, low, high):
        p_re, p_im = planes(it, m)
        batch = plan.batch if it == 0 else plan.wide

        def some(b, _):
            add_re = jnp.zeros((window, window), f32)
            add_im = jnp.zeros((window, window), f32)
            for v in range(batch):
                u = b * batch + v
                factor = power_ref[u]
                mid = left(left_t[1], far[m, u] * jnp.concatenate([factor, factor], axis=0))
                back = right(jnp.concatenate(turn([mid]), axis=0), right_t[1])
                for r in range(2):
                    w_re, w_im = wave_w[2 * u + r, 0], wave_w[2 * u + r, 1]
                    line = slice(r * window, (r + 1) * window)
                    b_re, b_im = back[line, :window], back[line, window:]
                    add_re = add_re + (w_re * b_re + w_im * b_im)
                    add_im = add_im + (w_re * b_im - w_im * b_re)
                    g_re = p_re * b_re + p_im * b_im
                    g_im = p_re * b_im - p_im * b_re
                    gw[2 * u + r, 0] = jnp.where(m == 0, g_re, gw[2 * u + r, 0] + g_re)
                    gw[2 * u + r, 1] = jnp.where(m == 0, g_im, gw[2 * u + r, 1] + g_im)
            for k, add in enumerate((add_re, add_im)):
                add = add.reshape(tiles, 8, window)
                grad[k, m] = jnp.where(b == 0, add, grad[k, m] + add)
            return 0

        lax.fori_loop(low // batch, high // batch, some, 0)

    def shift(scale, low, high):
        def one(s, _):
            _, _, row_s, col_s = cut_of(s, lax.rem(s, cap))
            lane17 = lax.broadcasted_iota(jnp.int32, (tiles + 1, 8, window), 2)
            sub17 = lax.broadcasted_iota(jnp.int32, (tiles + 1, 8, window), 1)
            none = jnp.zeros((1, 8, window), f32)
            for k in range(2):
                turned = pltpu.roll((gw[s, k] * scale).reshape(tiles, 8, window), lax.rem(row_s, 8), 1)
                wide = jnp.where(
                    sub17 >= row_s,
                    jnp.concatenate([turned, none], axis=0),
                    jnp.concatenate([none, turned], axis=0),
                )
                wide = pltpu.roll(wide, lax.rem(col_s, window), 2)
                shifted[s, k, 1:tiles + 2, 1] = jnp.where(lane17 >= col_s, wide, 0.0)
                shifted[s, k, 1:tiles + 2, 2] = jnp.where(lane17 < col_s, wide, 0.0)
            return 0

        lax.fori_loop(low, high, one, 0, unroll=4)

    def deposit(now, low, high):
        def lines(b, _):
            rows = [2 * b, 2 * b + 1]
            acc = [[[now[k, i, j] for j in range(plan.col_blocks)] for k in range(2)] for i in rows]
            for s in range(plan.slots):
                row0 = cut_of(s, s % cap)[0]
                at = [jnp.where((i >= row0) & (i <= row0 + tiles), i - row0 + 1, 0) for i in rows]
                for j in range(plan.col_blocks):
                    c = col_tab[s * plan.col_blocks + j]
                    for n in range(2):
                        for k in range(2):
                            acc[n][k][j] = acc[n][k][j] + shifted[s, k, at[n], c]
            for n, i in enumerate(rows):
                for k in range(2):
                    for j in range(plan.col_blocks):
                        next_spec[k, i, j] = acc[n][k][j]
            return 0

        lax.fori_loop(low // 2, high // 2, lines, 0)

    def light_one(it, d):
        n = plan.light
        return remote(
            light.at[pl.ds(flip(ty, d) * n, n)], lt_in.at[it, d], ls.at[it, d], lr.at[it, d], ty_dev[d]
        )

    def light_two(it, d):
        return remote(lx_in.at[it, 0], lx_in.at[it, d], xs.at[it, d], xr.at[it, d], tx_dev[d])

    def light_three(it, d):
        return remote(lm_in.at[it, 0], lm_in.at[it, d], ms.at[it, d], mr.at[it, d], ty_dev[d])

    def lighting(it, stage):
        if stage == 0:
            for d in range(1, nty):
                light_one(it, d).start()
        elif stage == 1:
            mine = light[pl.ds(ty * plan.light, plan.light)]
            for d in range(1, nty):
                light_one(it, d).wait()
                mine = mine + lt_in[it, d]
            lx_in[it, 0] = mine
            for d in range(1, plan.ntx):
                light_two(it, d).start()
        elif stage == 2:
            mine = lx_in[it, 0]
            for d in range(1, plan.ntx):
                light_two(it, d).wait()
                mine = mine + lx_in[it, d]
            lm_in[it, 0] = jnp.max(mine, axis=0)
            for d in range(1, nty):
                light_three(it, d).start()
        else:
            for d in range(1, nty):
                light_three(it, d).wait()

    def owned(at):
        return at * chunk // tiles, lax.rem(at * chunk, tiles)

    def step_a(it, g):
        return remote(
            grad.at[1 - core, pl.ds(g * per, per)], half_in.at[it, g], cs.at[it, g], cr.at[it, g], mate
        )

    def step_b(it, g, j):
        m, t = owned(chip_at[j])
        return remote(
            part.at[it, g, m, pl.ds(t, chunk)], rs_in.at[it, g, j], rs.at[it, g, j], rr.at[it, g, j], chip_dev[j]
        )

    def step_c(it, g, j):
        m, t = owned(chip)
        ref = probe.at[it + 1, core, g * per + m, pl.ds(t, chunk)]
        return remote(ref, ref, gs.at[it, g, j], gr.at[it, g, j], chip_dev[j])

    def step_d(it, g):
        ref = probe.at[it + 1, core, pl.ds(g * per, per)]
        return remote(ref, ref, bs.at[it, g], br.at[it, g], mate)

    def do_b(it, g):
        step_a(it, g).wait_recv()
        part[it, g] = grad[core, pl.ds(g * per, per)] + half_in[it, g]
        for j in range(len(chips)):
            step_b(it, g, j).start()

    def do_c(it, g, bottom):
        m, t = owned(chip)
        total = part[it, g, m, pl.ds(t, chunk)]
        for j in range(len(chips)):
            step_b(it, g, j).wait_recv()
            total = total + rs_in[it, g, j]
        at = g * per + m
        probe[it + 1, core, at, pl.ds(t, chunk)] = probe[it, core, at, pl.ds(t, chunk)] + total / bottom
        for j in range(len(chips)):
            step_c(it, g, j).start()

    def do_d(it, g):
        for j in range(len(chips)):
            step_c(it, g, j).wait_recv()
        step_d(it, g).start()

    def do_e(it, g):
        step_d(it, g).wait_recv()

    def close_a(it):
        for g in range(groups):
            step_a(it, g).wait_send()

    def close_b(it):
        def one(g, _):
            for j in range(len(chips)):
                step_b(it, g, j).wait_send()
            return 0

        lax.fori_loop(0, groups, one, 0)

    def close_c(it):
        def one(g, _):
            for j in range(len(chips)):
                step_c(it, g, j).wait_send()
            return 0

        lax.fori_loop(0, groups, one, 0)

    def close_d(it):
        for g in range(groups):
            step_d(it, g).wait_send()

    windows(spec)
    lighting(0, 0)
    for it in range(ITERS):
        now = spec if it == 0 else next_spec

        def ahead(m, _):
            if it:
                g = m // per

                @pl.when(lax.rem(m, per) == 0)
                def _():
                    @pl.when(g + 1 < groups)
                    def _():
                        do_d(it - 1, g + 1)

                    do_e(it - 1, g)

            forward(it, m)
            return 0

        lax.fori_loop(0, modes, ahead, 0)
        if it:
            lighting(it, 1)
            close_a(it - 1)

        scale = scale_of(it)

        def back(low, high, m, _):
            backward(it, m, low, high)
            g = m // per

            @pl.when(lax.rem(m, per) == per - 1)
            def _():
                step_a(it, g).start()

                @pl.when(g > 0)
                def _():
                    do_b(it, g - 1)

            @pl.when(m == modes // 2)
            def _():
                lighting(it, 2)

            return 0

        if it == 0:
            half = plan.units // 2
            factors(it, 0, half)

            def early(m, _):
                backward(it, m, 0, half)
                return 0

            lax.fori_loop(0, modes, early, 0)
            lighting(it, 1)
            factors(it, half, plan.units)
            lax.fori_loop(0, modes, functools.partial(back, half, plan.units), 0)
        else:
            factors(it, 0, plan.units)
            lax.fori_loop(0, modes, functools.partial(back, 0, plan.units), 0)
        shift(scale, 0, plan.slots // 2)
        do_b(it, groups - 1)
        shift(scale, plan.slots // 2, plan.slots)
        deposit(now, 0, plan.row_blocks // 4)
        lighting(it, 3)
        bottom = jnp.max(jnp.max(lm_in[it], axis=0), keepdims=True) + SMALL_EPS
        for g in range(groups):
            if g == groups // 2:
                deposit(now, plan.row_blocks // 4, plan.row_blocks // 2)
            do_c(it, g, bottom)
        deposit(now, plan.row_blocks // 2, plan.row_blocks)
        if it + 1 < ITERS:
            windows(next_spec)
            lighting(it + 1, 0)
            do_d(it, 0)
    it = ITERS - 1
    store = [
        pltpu.make_async_copy(
            next_spec.at[:, :, j], spec_out.at[:, :, :, pl.ds(j * window, window)], out_sem.at[2 + j]
        )
        for j in range(plan.col_blocks)
    ]
    for copy in store:
        copy.start()
    for copy in pats:
        copy.wait_send()
    for old in range(it):
        close_b(old)
        close_c(old)
        close_d(old)
    close_a(it)
    close_b(it)
    for g in range(groups):
        do_d(it, g)
    close_c(it)
    for g in range(groups):
        do_e(it, g)
    final = [
        pltpu.make_async_copy(probe.at[ITERS, k], probe_out.at[:, k], out_sem.at[k]) for k in range(2)
    ]
    for copy in final:
        copy.start()
    close_d(it)
    for copy in store + final:
        copy.wait()


def hand_over_kernel(spec_in, probe_in, spec_out, probe_out, spec, probe, sems):
    lines = spec_in.shape[1] // PARTS
    copies = []
    for k in range(2):
        for n in range(PARTS):
            at = pl.ds(n * lines, lines)
            copies.append((spec_in.at[k, at], spec.at[k, at], spec_out.at[k, at]))
    for m in range(probe_in.shape[0]):
        copies.append((probe_in.at[m], probe.at[m], probe_out.at[m]))
    inward = [pltpu.make_async_copy(a, b, sems.at[0, n]) for n, (a, b, _) in enumerate(copies)]
    outward = [pltpu.make_async_copy(b, c, sems.at[1, n]) for n, (_, b, c) in enumerate(copies)]
    for copy in inward:
        copy.start()
    for first, second in zip(inward, outward):
        first.wait()
        second.start()
    for copy in outward:
        copy.wait()


def shards(specimen, probe_modes, patterns, tile_row, row_offset, col_offset):
    own, window, _ = patterns.shape
    modes = probe_modes.shape[0]
    nty, ntx = lax.axis_size("ty"), lax.axis_size("tx")
    plan = Plan(nty, ntx, own, window, modes, specimen.shape[1], specimen.shape[2])
    lefts, rights = dft_tables(window)
    f32, dma = jnp.float32, pltpu.SemaphoreType.DMA
    shape = specimen.shape
    view = (2, plan.row_blocks, 8, shape[2])
    spec_view = (2, plan.row_blocks, plan.col_blocks, 8, window)
    tiles, cap, groups, others = plan.tiles, plan.cap, plan.groups, plan.chips - 1
    plane = (tiles, 8, window)
    probe_view = (modes, 2) + plane
    both = lambda *n: dma((ITERS,) + n)
    scratch = [
        VMEM(patterns.shape, f32),
        VMEM(spec_view, f32),
        VMEM(spec_view, f32),
        VMEM(lefts.shape, jnp.bfloat16),
        VMEM(rights.shape, jnp.bfloat16),
        VMEM((ITERS + 1, 2, modes) + plane, f32),
        VMEM((2, modes) + plane, f32),
        VMEM(plane, f32),
        VMEM((plan.slots, 2, tiles + 2, 3, 8, window), f32),
        VMEM((nty, cap, window, window), f32),
        VMEM((nty, cap, window, window), f32),
        VMEM((nty, 8, window), jnp.int32),
        VMEM((nty, 8, window), jnp.int32),
        SMEM((nty, 8, window), jnp.int32),
        SMEM((plan.slots * plan.col_blocks,), jnp.int32),
        VMEM((plan.slots, 2, window, window), f32),
        VMEM((modes, plan.units, 2 * window, 2 * window), f32),
        VMEM((plan.units, window, 2 * window), f32),
        VMEM((plan.slots, 2, window, window), f32),
        VMEM((ITERS, groups, plan.per) + plane, f32),
        VMEM((ITERS, groups, plan.per) + plane, f32),
        VMEM((ITERS, groups, others, plan.chunk, 8, window), f32),
        VMEM((ITERS, nty, plan.light, 8, window), f32),
        VMEM((ITERS, ntx, plan.light, 8, window), f32),
        VMEM((ITERS, nty, 8, window), f32),
        dma((5 + plan.col_blocks,)), dma((1,)), dma((2 + plan.col_blocks,)),
        dma((nty,)), dma((nty,)), dma((nty,)), dma((nty,)),
        both(nty), both(nty), both(ntx), both(ntx), both(nty), both(nty),
        both(groups), both(groups), both(groups, others), both(groups, others),
        both(groups, others), both(groups, others), both(groups), both(groups),
    ]
    out, probe = pl.pallas_call(
        functools.partial(program_kernel, plan),
        out_shape=(jax.ShapeDtypeStruct(view, f32), jax.ShapeDtypeStruct(probe_view, f32)),
        in_specs=[pl.BlockSpec(memory_space=SMEM)] * 3 + [pl.BlockSpec(memory_space=pl.ANY)] * 5,
        out_specs=(pl.BlockSpec(memory_space=pl.ANY),) * 2,
        scratch_shapes=scratch,
        compiler_params=pltpu.CompilerParams(
            collective_id=0, has_side_effects=True, vmem_limit_bytes=LIMIT
        ),
        name="program",
    )(
        tile_row, row_offset, col_offset, patterns, specimen.reshape(view),
        probe_modes.reshape(probe_view), jnp.asarray(lefts), jnp.asarray(rights),
    )
    out, probe = pl.pallas_call(
        hand_over_kernel,
        out_shape=(jax.ShapeDtypeStruct(view, f32), jax.ShapeDtypeStruct(probe_view, f32)),
        in_specs=[pl.BlockSpec(memory_space=pl.ANY)] * 2,
        out_specs=(pl.BlockSpec(memory_space=pl.ANY),) * 2,
        scratch_shapes=[VMEM(view, f32), VMEM(probe_view, f32), dma((2, 2 * PARTS + modes))],
        name="hand_over",
    )(out, probe)
    return out.reshape(shape), probe.reshape(probe_modes.shape)


def solution(mesh):
    placed = (
        P(None, "ty", "tx"),
        P(),
        P(("ty", "tx"), None, None),
        P(("ty", "tx")),
        P(("ty", "tx")),
        P(("ty", "tx")),
    )
    return jax.shard_map(
        shards, mesh=mesh, in_specs=placed, out_specs=(P(None, "ty", "tx"), P()), check_vma=False
    )
```
